32 devices in a mesh: energy: 8 (over z, core), momentum: 4 (over y, x).
Axes of the slice: x: 2, y: 2, z: 4, core: 2. Of those that a mesh axis runs over, the one named last changes fastest.
Arguments:
- hopping: float32 [4, 2, 2, 384, 384], P('momentum'), may hold values from -0.07 to 0.07, as said below
- coupling: float32 [4, 2, 384, 384], P('momentum'), may hold values from -0.15 to 0.15
- onsite: float32 [2, 384], replicated, may hold values from -4 to -2.5
- sigma_in: float32 [8, 4, 2, 147456], P('energy', 'momentum'), may hold values from -0.12 to 0.12
- neighbor_shift: int32 [96, 48], replicated, may hold values from 1 to 95
- mode_shift: int32 [6], replicated, may hold values from 1 to 3
- phonon_kernel: float32 [6, 2, 4, 4], replicated, may hold values from -240 to 240
Outputs:
- sigma_new: float32 [8, 4, 2, 147456], P('energy', 'momentum')
The draws below stay inside these ranges and needn't reach their ends.
Inputs may be any that keep to these rules, and one draw needn't show every extreme that they name: hopping[k, c, 0] is symmetric with a zero diagonal and hopping[k, c, 1] is antisymmetric, so every cell block is Hermitian.
All inputs are finite; a program needn't handle non-finite values.
Results may differ from the reference program's by a relative error of at most 0.0003.
Values sent between devices are 32-bit elements; how exact they have to be, the bound alone decides.
A program may use at most 256 MiB of HBM per device.

```python
import jax
import jax.numpy as jnp
from jax import lax

ORB = 384
ORB_ATOM = 4
ATOMS = 96
NEIGH = 48
PAIR_COLS = 147456
MODES = 6
NS_STEPS = 2
ENERGIES = 8
MOMENTA = 4


def draw_hopping(key, part):
    first_key, second_key = jax.random.split(jax.random.fold_in(key, 11))
    array_shape = (MOMENTA, 2, ORB, ORB)
    real_draw = jax.random.uniform(first_key, array_shape, jnp.float32, -0.07, 0.07)
    imag_draw = jax.random.uniform(second_key, array_shape, jnp.float32, -0.07, 0.07)
    row_index = lax.broadcasted_iota(jnp.int32, (ORB, ORB), 0)
    col_index = lax.broadcasted_iota(jnp.int32, (ORB, ORB), 1)
    off_diagonal = (row_index != col_index).astype(jnp.float32)
    real_part = 0.5 * (real_draw + jnp.swapaxes(real_draw, -1, -2)) * off_diagonal
    imag_part = 0.5 * (imag_draw - jnp.swapaxes(imag_draw, -1, -2))
    return jnp.stack([real_part, imag_part], axis=2)


def draw_coupling(key, part):
    first_key = jax.random.fold_in(jax.random.fold_in(key, 23), 0)
    array_shape = (MOMENTA, 2, ORB, ORB)
    entries = 0.025 * jax.random.normal(first_key, array_shape, jnp.float32)
    return jnp.clip(entries, -0.15, 0.15)


def place_ends(array, key, low, high):
    shape = array.shape
    spot = [jax.random.randint(jax.random.fold_in(key, axis), (), 0, shape[axis]) for axis in range(len(shape))]
    array = array.at[tuple(spot)].set(low)
    longest = shape.index(max(shape))
    spot[longest] = (spot[longest] + 1) % shape[longest]
    return array.at[tuple(spot)].set(high)


def block_scale(rng, shape, pieces, smallest, largest):
    def one(position, parts):
        steps = jax.random.uniform(jax.random.fold_in(jax.random.fold_in(rng, 6), position), (parts,), jnp.float32, smallest / len(pieces), largest / len(pieces))
        return jnp.repeat(jnp.exp(steps), shape[position] // parts).reshape((-1,) + (1,) * (len(shape) - position - 1))

    loudness = one(*pieces[0])
    for cut in pieces[1:]:
        loudness = loudness * one(*cut)
    return loudness


def centred(key, shape, deviation, limit, cuts=(), kind=jnp.bfloat16):
    level = block_scale(key, shape, cuts, -0.22, 0.18) if cuts else 1.0
    result = jax.random.normal(key, shape, jnp.float32) * deviation * level
    return jnp.minimum(jnp.maximum(result, -limit), limit).astype(kind)


def setup_inputs(seed: int = 0) -> dict:
    key_of = jax.random.split(jax.random.key(seed), 8)
    return {
        "hopping": draw_hopping(jax.random.fold_in(key_of[7], 71), 0),
        "coupling": draw_coupling(jax.random.fold_in(key_of[7], 71), 0),
        "onsite": jnp.clip(jax.random.uniform(key_of[2], (2, ORB), jnp.float32, -4.0, -2.5), -4.0, -2.5),
        "sigma_in": centred(key_of[3], (ENERGIES, MOMENTA, 2, PAIR_COLS), 0.02, 0.12, ((0, 8), (1, 4)), jnp.float32),
        "neighbor_shift": place_ends(jax.random.randint(key_of[4], (ATOMS, NEIGH), 1, ATOMS), jax.random.fold_in(key_of[4], 1), 1, ATOMS - 1).astype(jnp.int32),
        "mode_shift": place_ends(jax.random.randint(key_of[5], (MODES,), 1, ENERGIES // 2), jax.random.fold_in(key_of[5], 1), 1, (ENERGIES // 2) - 1).astype(jnp.int32),
        "phonon_kernel": centred(key_of[6], (MODES, 2, MOMENTA, MOMENTA), 40.0, 240.0, (), jnp.float32),
    }


BROADENING = 0.5


def matmul_high(first_matrix, second_matrix):
    return jnp.dot(first_matrix, second_matrix, precision=lax.Precision.HIGHEST, preferred_element_type=jnp.float32)


def complex_product(first_pair, second_pair):
    real_real = matmul_high(first_pair[0], second_pair[0])
    imag_imag = matmul_high(first_pair[1], second_pair[1])
    summed = matmul_high(first_pair[0] + first_pair[1], second_pair[0] + second_pair[1])
    return (real_real - imag_imag, summed - real_real - imag_imag)


def newton_inverse(system):
    diagonal_real = jnp.diagonal(system[0])
    diagonal_imag = jnp.diagonal(system[1])
    magnitude = diagonal_real * diagonal_real + diagonal_imag * diagonal_imag
    inverse_real = diagonal_real / magnitude
    inverse_imag = -diagonal_imag / magnitude
    column_real = system[0] * inverse_real[None, :] - system[1] * inverse_imag[None, :]
    column_imag = system[0] * inverse_imag[None, :] + system[1] * inverse_real[None, :]
    scaled_real = inverse_real[:, None] * column_real - inverse_imag[:, None] * column_imag
    scaled_imag = inverse_real[:, None] * column_imag + inverse_imag[:, None] * column_real
    guess = (2.0 * jnp.diag(inverse_real) - scaled_real, 2.0 * jnp.diag(inverse_imag) - scaled_imag)
    for step_number in range(NS_STEPS - 1):
        product = complex_product(system, guess)
        correction = complex_product(guess, product)
        guess = (2.0 * guess[0] - correction[0], 2.0 * guess[1] - correction[1])
    return guess


def place_pairs(pair_values, row_atom, col_atom):
    entries = pair_values.reshape(ATOMS, NEIGH, 2, ORB_ATOM, ORB_ATOM)
    placed = jnp.zeros((2, ATOMS, ORB_ATOM, ATOMS, ORB_ATOM), jnp.float32).at[:, row_atom, :, col_atom, :].add(entries)
    placed = placed.reshape(2, ORB, ORB)
    return (placed[0], placed[1])


def pick_pairs(matrix_pair, row_atom, col_atom):
    stacked = jnp.stack([matrix_pair[0], matrix_pair[1]]).reshape(2, ATOMS, ORB_ATOM, ATOMS, ORB_ATOM)
    return stacked[:, row_atom, :, col_atom, :].reshape(PAIR_COLS)


def green_point(energy_real, hopping_block, coupling_block, onsite, sigma_point, row_atom, col_atom):
    identity = jnp.eye(ORB, dtype=jnp.float32)
    systems = []
    for cell_index in range(2):
        self_energy = place_pairs(sigma_point[cell_index], row_atom, col_atom)
        system_real = jnp.diag(energy_real - onsite[cell_index]) - hopping_block[cell_index, 0] - self_energy[0]
        system_imag = BROADENING * identity - hopping_block[cell_index, 1] - self_energy[1]
        systems.append((system_real, system_imag))
    first_green = newton_inverse(systems[0])
    coupling_pair = (coupling_block[0], coupling_block[1])
    coupling_adjoint = (coupling_block[0].T, -coupling_block[1].T)
    adjoint_green = complex_product(coupling_adjoint, first_green)
    folded = complex_product(adjoint_green, coupling_pair)
    second_green = newton_inverse((systems[1][0] - folded[0], systems[1][1] - folded[1]))
    green_coupling = complex_product(first_green, coupling_pair)
    through = complex_product(complex_product(green_coupling, second_green), adjoint_green)
    first_full = (first_green[0] + through[0], first_green[1] + through[1])
    return jnp.stack([pick_pairs(first_full, row_atom, col_atom), pick_pairs(second_green, row_atom, col_atom)])


def build_kernel(mode_shift, phonon_kernel, energies, momenta):
    target = lax.broadcasted_iota(jnp.int32, (MODES, energies, energies), 1)
    source = lax.broadcasted_iota(jnp.int32, (MODES, energies, energies), 2)
    shifted = mode_shift[:, None, None]
    lower = (source == target - shifted).astype(jnp.float32)
    upper = (source == target + shifted).astype(jnp.float32)
    combined = jnp.einsum("jab,jkq->akbq", lower, phonon_kernel[:, 0], precision=lax.Precision.HIGHEST)
    combined = combined + jnp.einsum("jab,jkq->akbq", upper, phonon_kernel[:, 1], precision=lax.Precision.HIGHEST)
    return combined.reshape(energies * momenta, energies * momenta)


def reference(hopping, coupling, onsite, sigma_in, neighbor_shift, mode_shift, phonon_kernel):
    row_atom = lax.broadcasted_iota(jnp.int32, (ATOMS, NEIGH), 0)
    col_atom = (row_atom + neighbor_shift) % ATOMS

    def one_point(point_index):
        energy = point_index // MOMENTA
        momentum = point_index % MOMENTA
        energy_real = 2.0 * (energy.astype(jnp.float32) + 0.5) / ENERGIES
        return green_point(energy_real, hopping[momentum], coupling[momentum], onsite, sigma_in[energy, momentum], row_atom, col_atom)

    green_pairs = lax.map(one_point, jnp.arange(ENERGIES * MOMENTA, dtype=jnp.int32))
    kernel = build_kernel(mode_shift, phonon_kernel, ENERGIES, MOMENTA)
    flattened = green_pairs.reshape(ENERGIES * MOMENTA, 2 * PAIR_COLS)
    return matmul_high(kernel, flattened).reshape(ENERGIES, MOMENTA, 2, PAIR_COLS)
```

```python
import functools

import jax
import jax.numpy as jnp
from jax import lax
from jax.experimental import pallas as pl
from jax.experimental.pallas import tpu as pltpu
from jax.sharding import PartitionSpec as P

BROADENING = 0.5
LANES = 128
F32 = jnp.float32
BF16 = jnp.bfloat16


def dot(a, b):
    return jnp.dot(a, b, preferred_element_type=F32)


def split(x):
    high = x.astype(BF16)
    return high, (x - high.astype(F32)).astype(BF16)


def point_kernel(
    dims, z_ref, pairs_ref, shift_ref, hop_ref, coup_ref, onsite_ref, out_ref,
    rows_ref, sig_ref, acc_ref, coupling, adjoint, system, guess, prod, first, second, ag,
    left_h, left_l, right_h, right_l,
):
    atoms, neigh, per_atom = dims
    orb = atoms * per_atom
    entries = 2 * per_atom * per_atom
    groups = LANES // entries
    chunks = neigh // groups
    f32_lanes = lax.broadcasted_iota(jnp.int32, (atoms, LANES), 1)

    for cell in range(2):
        for chunk in range(chunks):
            part = pairs_ref[pl.ds(2 * chunk + cell, atoms, stride=2 * chunks), :]
            rows_ref[chunk * LANES:(chunk + 1) * LANES, 0:atoms] = part.T
        for entry in range(entries):
            part = rows_ref[pl.ds(entry, neigh, stride=entries), :]
            sig_ref[cell * entries + entry, :, 0:neigh] = part.T[0:atoms]

    index = lax.broadcasted_iota(jnp.int32, (atoms, neigh), 0) + shift_ref[...].T
    index = jnp.where(index >= atoms, index - atoms, index)

    def following(previous):
        current = jnp.full((atoms, LANES), LANES, jnp.int32)
        for n in reversed(range(neigh)):
            column = jnp.broadcast_to(index[:, n:n + 1], (atoms, LANES))
            current = jnp.where((column == f32_lanes) & (n > previous), n, current)
        return current

    def gathered(block, current):
        safe = jnp.where(current < LANES, current, 0)
        value = jnp.take_along_axis(sig_ref[block], safe, axis=1)
        return jnp.where(current < LANES, value, 0.0)

    def smallest(current):
        return jnp.min(current)

    current = following(jnp.full((atoms, LANES), -1, jnp.int32))

    unroll = 8

    def store_first(group, carry):
        for u in range(unroll):
            block = group * unroll + u
            acc_ref[block] = gathered(block, current)
        return carry

    lax.fori_loop(0, 2 * entries // unroll, store_first, 0)

    def more(state):
        return state[1] < LANES

    def step(state):
        now = state[0]

        def add(group, carry):
            for u in range(unroll):
                block = group * unroll + u
                acc_ref[block] = acc_ref[block] + gathered(block, now)
            return carry

        lax.fori_loop(0, 2 * entries // unroll, add, 0)
        later = following(now)
        return later, smallest(later)

    current = following(current)
    lax.while_loop(more, step, (current, smallest(current)))

    row = lax.broadcasted_iota(jnp.int32, (orb, orb), 0)
    col = lax.broadcasted_iota(jnp.int32, (orb, orb), 1)
    eye = row == col

    def source(position):
        turn = sum((position >= atoms * k).astype(jnp.int32) for k in range(1, per_atom))
        return per_atom * (position - atoms * turn) + turn

    perm = (col == source(row)).astype(F32).astype(BF16)
    perm_t = (row == source(col)).astype(F32).astype(BF16)

    def permuted(matrix):
        high, low = split(matrix)
        moved = dot(perm, jnp.concatenate([high, low], axis=1)).astype(BF16)
        return dot(moved[:, 0:orb], perm_t) + dot(moved[:, orb:], perm_t)

    def put_left(ref):
        high, low = split(ref[...])
        left_h[...] = high
        left_l[...] = low

    def put_right(ref):
        high, low = split(ref[...])
        for part, dst in ((high, right_h), (low, right_l)):
            dst[0:orb, :] = part
            dst[orb:2 * orb, 0:orb] = -part[:, orb:]
            dst[orb:2 * orb, orb:] = part[:, 0:orb]

    width = 256 if (2 * orb) % 256 == 0 else LANES

    def product(emit):
        for t in range(2 * orb // width):
            window = slice(t * width, (t + 1) * width)
            high = right_h[:, window]
            total = dot(left_h[...], right_l[:, window]) + dot(left_l[...], high)
            emit(window, total + dot(left_h[...], high))

    def into(dst):
        def emit(window, value):
            dst[:, window] = value
        return emit

    def invert(dst):
        real, imag = system[:, 0:orb], system[:, orb:]
        own_real, own_imag = jnp.where(eye, real, 0.0), jnp.where(eye, imag, 0.0)
        pairs = []
        for axis in (0, 1):
            dr = jnp.sum(own_real, axis=axis, keepdims=True)
            di = jnp.sum(own_imag, axis=axis, keepdims=True)
            size = dr * dr + di * di
            pairs.append((dr / size, -di / size))
        (rr, ri), (cr, ci) = pairs
        col_real, col_imag = real * rr - imag * ri, real * ri + imag * rr
        guess[:, 0:orb] = jnp.where(eye, 2.0 * rr, 0.0) - (cr * col_real - ci * col_imag)
        guess[:, orb:] = jnp.where(eye, 2.0 * ri, 0.0) - (cr * col_imag + ci * col_real)
        put_left(system)
        put_right(guess)
        product(into(prod))
        put_left(guess)
        put_right(prod)

        def emit(window, value):
            dst[:, window] = 2.0 * guess[:, window] - value

        product(emit)

    def build_system(cell):
        onsite = jnp.where(eye, onsite_ref[cell:cell + 1, :], 0.0)
        system[:, 0:orb] = jnp.where(eye, z_ref[0], 0.0) - permuted(hop_ref[0, cell, 0] + onsite)
        system[:, orb:] = jnp.where(eye, BROADENING, 0.0) - permuted(hop_ref[0, cell, 1])
        for part in range(2):
            for i in range(per_atom):
                blocks = []
                for j in range(per_atom):
                    entry = ((cell * 2 + part) * per_atom + i) * per_atom + j
                    blocks.append(acc_ref[entry][:, 0:atoms])
                band = (slice(i * atoms, (i + 1) * atoms), slice(part * orb, (part + 1) * orb))
                system[band] = system[band] - jnp.concatenate(blocks, axis=1)

    coup_real, coup_imag = permuted(coup_ref[0, 0]), permuted(coup_ref[0, 1])
    coupling[:, 0:orb] = coup_real
    coupling[:, orb:] = coup_imag
    adjoint[:, 0:orb] = coup_real.T
    adjoint[:, orb:] = -coup_imag.T

    build_system(0)
    invert(first)
    put_left(adjoint)
    put_right(first)
    product(into(ag))
    build_system(1)
    put_left(ag)
    put_right(coupling)

    def fold(window, value):
        system[:, window] = system[:, window] - value

    product(fold)
    put_left(first)
    product(into(adjoint))
    invert(second)
    put_left(adjoint)
    put_right(second)
    product(into(prod))
    put_left(prod)
    put_right(ag)

    def full(window, value):
        first[:, window] = first[:, window] + value

    product(full)

    pad = jnp.zeros((atoms, LANES - neigh), jnp.int32)
    pick = jnp.concatenate([index, pad], axis=1)
    for cell, green in ((0, first), (1, second)):
        for part in range(2):
            for i in range(per_atom):
                for j in range(per_atom):
                    start = part * orb + j * atoms
                    lane = min(start, 2 * orb - LANES)
                    block = green[i * atoms:(i + 1) * atoms, lane:lane + LANES]
                    value = jnp.take_along_axis(block, pick + (start - lane), axis=1)
                    entry = (part * per_atom + i) * per_atom + j
                    value = jnp.concatenate([value, jnp.zeros((LANES - atoms, LANES), F32)], axis=0)
                    rows_ref[pl.ds(entry, neigh, stride=entries), :] = value.T[0:neigh]
        for chunk in range(chunks):
            part = rows_ref[chunk * LANES:(chunk + 1) * LANES, :].T
            out_ref[cell, pl.ds(chunk, atoms, stride=chunks), :] = part[0:atoms]


def green_pairs_of(energy_real, pairs, neighbor_shift, hopping, coupling, onsite, per_atom):
    neigh, atoms = neighbor_shift.shape
    orb = atoms * per_atom
    entries = 2 * per_atom * per_atom
    vmem = pl.BlockSpec(memory_space=pltpu.VMEM)
    complex_block = pltpu.VMEM((orb, 2 * orb), F32)
    return pl.pallas_call(
        functools.partial(point_kernel, (atoms, neigh, per_atom)),
        out_shape=jax.ShapeDtypeStruct((2, pairs.shape[0] // 2, LANES), F32),
        in_specs=[pl.BlockSpec(memory_space=pltpu.SMEM)] + [vmem] * 5,
        out_specs=vmem,
        scratch_shapes=[
            pltpu.VMEM((neigh * entries, LANES), F32),
            pltpu.VMEM((2 * entries, atoms, LANES), F32),
            pltpu.VMEM((2 * entries, atoms, LANES), F32),
        ]
        + [complex_block] * 8
        + [pltpu.VMEM((orb, 2 * orb), BF16)] * 2
        + [pltpu.VMEM((2 * orb, 2 * orb), BF16)] * 2,
        compiler_params=pltpu.CompilerParams(vmem_limit_bytes=60 * 1024 * 1024),
        name="point_green",
    )(energy_real, pairs, neighbor_shift, hopping, coupling, onsite)


MESH = pl.DeviceIdType.MESH


class Exchange:
    def __init__(self, dims, green, out, field, mixed, table, sems):
        self.energies, self.momenta, self.chunks, self.order = dims
        self.green, self.out, self.field, self.mixed, self.table = green, out, field, mixed, table
        self.plane_send, self.plane_recv, self.hop_send, self.hop_recv, self.back_send, self.back_recv = sems
        self.plane = 2 * self.momenta
        self.span = self.energies // 2 - 1
        self.reach = (self.span + 1) // 2
        self.groups = self.energies // 2
        self.steps = [(cell, chunk) for cell in self.order for chunk in range(self.chunks)]
        energy, self.k = lax.axis_index("energy"), lax.axis_index("momentum")
        self.group, self.core = energy // 2, energy % 2
        self.me = self.core * self.momenta + self.k

    def member(self, index):
        return (2 * self.group + index // self.momenta, index % self.momenta)

    def partner(self, turn):
        return lax.rem(self.me + turn, self.plane)

    def beside(self, side):
        return (jnp.clip(2 * (self.group + side), 0, self.energies - 2) + self.core, self.k)

    def has(self, side, hops=1):
        other = self.group + side * hops
        return (other >= 0) & (other < self.groups)

    def parts(self, hop):
        near = 2 * hop - 1 <= self.span
        far = 2 * hop <= self.span
        return near, far

    def announce(self):
        barrier = pltpu.get_barrier_semaphore()
        for turn in range(1, self.plane):
            pl.semaphore_signal(barrier, inc=1, device_id=self.member(self.partner(turn)), device_id_type=MESH)
        for side in (-1, 1):
            @pl.when(self.has(side))
            def _():
                pl.semaphore_signal(barrier, inc=1, device_id=self.beside(side), device_id_type=MESH)

    def greeted(self):
        count = self.plane - 1 + self.has(-1).astype(jnp.int32) + self.has(1).astype(jnp.int32)
        pl.semaphore_wait(pltpu.get_barrier_semaphore(), count)

    def blank(self):
        for side in (-1, 1):
            for hop in range(1, self.reach + 1):
                @pl.when(jnp.logical_not(self.has(side, hop)))
                def _():
                    for t in range(len(self.steps)):
                        shape = self.field.shape[2:]
                        self.field[t, self.reach + side * hop] = jnp.zeros(shape, F32)

    def plane_copy(self, t, turn):
        cell, chunk = self.steps[t]
        other = self.partner(turn)
        return pltpu.make_async_remote_copy(
            src_ref=self.green.at[cell, chunk, other],
            dst_ref=self.field.at[t, self.reach, self.me],
            send_sem=self.plane_send.at[t, turn],
            recv_sem=self.plane_recv.at[t, turn],
            device_id=self.member(other),
            device_id_type=MESH,
        )

    def plane_start(self, t):
        for turn in range(1, self.plane):
            self.plane_copy(t, turn).start()
        cell, chunk = self.steps[t]
        self.field[t, self.reach, self.me] = self.green[cell, chunk, self.me]

    def plane_wait(self, t):
        for turn in range(1, self.plane):
            self.plane_copy(t, turn).wait()

    def hop_copy(self, t, side, hop, half):
        place = self.reach - side * (hop - 1)
        rows = pl.ds(half * self.momenta, self.momenta)
        index = 0 if side < 0 else 1
        return pltpu.make_async_remote_copy(
            src_ref=self.field.at[t, place, rows],
            dst_ref=self.field.at[t, place - side, rows],
            send_sem=self.hop_send.at[t, index, hop - 1, half],
            recv_sem=self.hop_recv.at[t, index, hop - 1, half],
            device_id=self.beside(side),
            device_id_type=MESH,
        )

    def halves(self, side, hop):
        near, far = self.parts(hop)
        first = 1 if side > 0 else 0
        return [half for half, used in ((first, near), (1 - first, far)) if used]

    def sends(self, side, hop):
        return self.has(side) & self.has(-side, hop - 1)

    def hop_start(self, t, hop):
        for side in (-1, 1):
            @pl.when(self.sends(side, hop))
            def _():
                for half in self.halves(side, hop):
                    self.hop_copy(t, side, hop, half).start()

    def hop_wait_recv(self, t, hop):
        for side in (-1, 1):
            @pl.when(self.has(-side, hop))
            def _():
                for half in self.halves(side, hop):
                    self.hop_copy(t, side, hop, half).wait_recv()

    def hop_wait_send(self, t, hop):
        for side in (-1, 1):
            @pl.when(self.sends(side, hop))
            def _():
                for half in self.halves(side, hop):
                    self.hop_copy(t, side, hop, half).wait_send()

    def weights(self, shift_ref, kernel_ref):
        modes = kernel_ref.shape[0] // 2
        points = self.momenta * self.momenta

        def entry(index, carry):
            values = [[kernel_ref[2 * m + way, index] for m in range(modes)] for way in range(2)]
            for way in range(2):
                for distance in range(1, self.span + 1):
                    total = jnp.float32(0.0)
                    for m in range(modes):
                        total = total + jnp.where(shift_ref[m] == distance, values[way][m], 0.0)
                    self.table[way * self.span + distance - 1, index] = total
            return carry

        lax.fori_loop(0, points, entry, 0)

    def mix(self, t):
        cell, chunk = self.steps[t]
        rows = self.field.shape[3]
        tile = 16 if rows % 16 == 0 else 8

        def block(index, carry):
            window = pl.ds(pl.multiple_of(index * tile, tile), tile)
            totals = [[None] * self.momenta for _ in range(2)]
            for offset in range(-self.reach, self.reach + 1):
                for half in range(2):
                    distances = [core - half - 2 * offset for core in range(2)]
                    if all(d == 0 or abs(d) > self.span for d in distances):
                        continue
                    for q in range(self.momenta):
                        value = self.field[t, self.reach + offset, half * self.momenta + q, window]
                        for core, d in enumerate(distances):
                            if d == 0 or abs(d) > self.span:
                                continue
                            row = (0 if d > 0 else self.span) + abs(d) - 1
                            for k in range(self.momenta):
                                term = self.table[row, k * self.momenta + q] * value
                                old = totals[core][k]
                                totals[core][k] = term if old is None else old + term
            for core in range(2):
                for k in range(self.momenta):
                    self.mixed[t, core * self.momenta + k, window] = totals[core][k]
            return carry

        lax.fori_loop(0, rows // tile, block, 0)

    def back_copy(self, t, turn):
        cell, chunk = self.steps[t]
        other = self.partner(turn)
        return pltpu.make_async_remote_copy(
            src_ref=self.mixed.at[t, other],
            dst_ref=self.out.at[cell, chunk, self.me],
            send_sem=self.back_send.at[t, turn],
            recv_sem=self.back_recv.at[t, turn],
            device_id=self.member(other),
            device_id_type=MESH,
        )

    def back_start(self, t):
        for turn in range(1, self.plane):
            self.back_copy(t, turn).start()
        cell, chunk = self.steps[t]
        self.out[cell, chunk, self.me] = self.mixed[t, self.me]

    def advance(self, s):
        last = len(self.steps)
        if s < last:
            self.plane_wait(s)
            self.hop_start(s, 1)
        for hop in range(2, self.reach + 1):
            t = s - (hop - 1)
            if 0 <= t < last:
                self.hop_wait_recv(t, hop - 1)
                self.hop_start(t, hop)
        t = s - self.reach
        if 0 <= t < last:
            self.hop_wait_recv(t, self.reach)
            self.mix(t)
            self.back_start(t)

    def finish(self):
        for t in range(len(self.steps)):
            for hop in range(1, self.reach + 1):
                self.hop_wait_send(t, hop)
            for turn in range(1, self.plane):
                self.back_copy(t, turn).wait()


def exchange_scratch(energies, momenta, steps, rows):
    plane, span = 2 * momenta, energies // 2 - 1
    reach = (span + 1) // 2
    dma = pltpu.SemaphoreType.DMA
    return [
        pltpu.VMEM((steps, 2 * reach + 1, plane, rows, LANES), F32),
        pltpu.VMEM((steps, plane, rows, LANES), F32),
        pltpu.SMEM((2 * span, momenta * momenta), F32),
        dma((steps, plane)), dma((steps, plane)),
        dma((steps, 2, reach, 2)), dma((steps, 2, reach, 2)),
        dma((steps, plane)), dma((steps, plane)),
    ]


def chunks_of(cell_rows, plane):
    for chunks in (3, 2, 1):
        if cell_rows % (chunks * plane * 8) == 0:
            return chunks
    raise ValueError("rows")


def exchange_kernel(dims, shift_ref, kernel_ref, green_ref, out_ref, field, mixed, table, *sems):
    ex = Exchange(dims, green_ref, out_ref, field, mixed, table, sems)
    ex.announce()
    ex.greeted()
    steps = len(ex.steps)
    ahead = min(2, steps)
    for t in range(ahead):
        ex.plane_start(t)
    ex.weights(shift_ref, kernel_ref)
    ex.blank()
    for s in range(steps + ex.reach):
        ex.advance(s)
        if s + ahead < steps:
            ex.plane_start(s + ahead)
    ex.finish()


def exchanged(green, mode_shift, phonon_kernel, energies, momenta):
    cells, chunks, plane, rows, _ = green.shape
    steps = cells * chunks
    smem, vmem = pl.BlockSpec(memory_space=pltpu.SMEM), pl.BlockSpec(memory_space=pltpu.VMEM)
    order = tuple(reversed(range(cells)))
    return pl.pallas_call(
        functools.partial(exchange_kernel, (energies, momenta, chunks, order)),
        out_shape=jax.ShapeDtypeStruct(green.shape, F32),
        in_specs=[smem, smem, vmem],
        out_specs=vmem,
        scratch_shapes=exchange_scratch(energies, momenta, steps, rows),
        compiler_params=pltpu.CompilerParams(
            collective_id=0, has_side_effects=True, vmem_limit_bytes=60 * 1024 * 1024
        ),
        name="exchange_points",
    )(mode_shift, phonon_kernel.reshape(-1, momenta * momenta), green)


def body(hopping, coupling, onsite, sigma_in, neighbor_shift, mode_shift, phonon_kernel):
    energies = sigma_in.shape[0] * lax.axis_size("energy")
    momenta = sigma_in.shape[1] * lax.axis_size("momentum")
    pair_cols = sigma_in.shape[3]
    atoms = neighbor_shift.shape[0]
    per_atom = onsite.shape[1] // atoms
    energy_real = 2.0 * (lax.axis_index("energy").astype(F32) + 0.5) / energies
    pairs = sigma_in.reshape(2, pair_cols // LANES, LANES).transpose(1, 0, 2)
    pairs = pairs.reshape(2 * pair_cols // LANES, LANES)
    green = green_pairs_of(
        energy_real.reshape(1), pairs, neighbor_shift.T, hopping, coupling, onsite, per_atom
    )
    cell_rows = pair_cols // LANES
    plane = 2 * momenta
    chunks = chunks_of(cell_rows, plane)
    green = green.reshape(2, chunks, plane, cell_rows // (chunks * plane), LANES)
    mixed = exchanged(green, mode_shift, phonon_kernel, energies, momenta)
    return mixed.reshape(1, 1, 2, pair_cols)


def solution(mesh):
    return jax.shard_map(
        body,
        mesh=mesh,
        in_specs=(
            P("momentum", None, None, None, None),
            P("momentum", None, None, None),
            P(),
            P("energy", "momentum", None, None),
            P(),
            P(),
            P(),
        ),
        out_specs=P("energy", "momentum", None, None),
        check_vma=False,
    )
```

```python
import functools

import jax
import jax.numpy as jnp
from jax import lax
from jax.experimental import pallas as pl
from jax.experimental.pallas import tpu as pltpu
from jax.sharding import PartitionSpec as P

BROADENING = 0.5
LANES = 128
F32 = jnp.float32
BF16 = jnp.bfloat16


MESH = pl.DeviceIdType.MESH


class Exchange:
    def __init__(self, dims, green, back, out, field, mixed, table, sems, store_sem):
        self.energies, self.momenta, self.chunks = dims
        self.green, self.back, self.out, self.field = green, back, out, field
        self.mixed, self.table, self.store_sem = mixed, table, store_sem
        self.plane_send, self.plane_recv, self.hop_send, self.hop_recv, self.back_send, self.back_recv = sems
        self.plane = 2 * self.momenta
        self.span = self.energies // 2 - 1
        self.reach = (self.span + 1) // 2
        self.groups = self.energies // 2
        self.steps = [(cell, chunk) for cell in (1, 0) for chunk in range(self.chunks)]
        energy, self.k = lax.axis_index("energy"), lax.axis_index("momentum")
        self.group, self.core = energy // 2, energy % 2
        self.me = self.core * self.momenta + self.k

    def member(self, index):
        return (2 * self.group + index // self.momenta, index % self.momenta)

    def partner(self, turn):
        return lax.rem(self.me + turn, self.plane)

    def beside(self, side):
        return (jnp.clip(2 * (self.group + side), 0, self.energies - 2) + self.core, self.k)

    def has(self, side, hops=1):
        other = self.group + side * hops
        return (other >= 0) & (other < self.groups)

    def parts(self, hop):
        near = 2 * hop - 1 <= self.span
        far = 2 * hop <= self.span
        return near, far

    def slot(self, chunk, owner):
        rows = self.field.shape[3]
        return pl.ds(pl.multiple_of((chunk * self.plane + owner) * rows, 8), rows)

    def announce(self):
        barrier = pltpu.get_barrier_semaphore()
        for turn in range(1, self.plane):
            pl.semaphore_signal(barrier, inc=1, device_id=self.member(self.partner(turn)), device_id_type=MESH)
        for side in (-1, 1):
            @pl.when(self.has(side))
            def _():
                pl.semaphore_signal(barrier, inc=1, device_id=self.beside(side), device_id_type=MESH)

    def greeted(self):
        count = self.plane - 1 + self.has(-1).astype(jnp.int32) + self.has(1).astype(jnp.int32)
        pl.semaphore_wait(pltpu.get_barrier_semaphore(), count)

    def blank(self):
        for side in (-1, 1):
            for hop in range(1, self.reach + 1):
                @pl.when(jnp.logical_not(self.has(side, hop)))
                def _():
                    for t in range(len(self.steps)):
                        shape = self.field.shape[2:]
                        self.field[t, self.reach + side * hop] = jnp.zeros(shape, F32)

    def plane_copy(self, t, turn):
        cell, chunk = self.steps[t]
        other = self.partner(turn)
        return pltpu.make_async_remote_copy(
            src_ref=self.green.at[cell, self.slot(chunk, other)],
            dst_ref=self.field.at[t, self.reach, self.me],
            send_sem=self.plane_send.at[t, turn],
            recv_sem=self.plane_recv.at[t, turn],
            device_id=self.member(other),
            device_id_type=MESH,
        )

    def plane_start(self, t):
        for turn in range(1, self.plane):
            self.plane_copy(t, turn).start()
        cell, chunk = self.steps[t]
        self.field[t, self.reach, self.me] = self.green[cell, self.slot(chunk, self.me)]

    def plane_wait(self, t):
        for turn in range(1, self.plane):
            self.plane_copy(t, turn).wait()

    def hop_copy(self, t, side, hop, half):
        place = self.reach - side * (hop - 1)
        rows = pl.ds(half * self.momenta, self.momenta)
        index = 0 if side < 0 else 1
        return pltpu.make_async_remote_copy(
            src_ref=self.field.at[t, place, rows],
            dst_ref=self.field.at[t, place - side, rows],
            send_sem=self.hop_send.at[t, index, hop - 1, half],
            recv_sem=self.hop_recv.at[t, index, hop - 1, half],
            device_id=self.beside(side),
            device_id_type=MESH,
        )

    def halves(self, side, hop):
        near, far = self.parts(hop)
        first = 1 if side > 0 else 0
        return [half for half, used in ((first, near), (1 - first, far)) if used]

    def sends(self, side, hop):
        return self.has(side) & self.has(-side, hop - 1)

    def hop_start(self, t, hop):
        for side in (-1, 1):
            @pl.when(self.sends(side, hop))
            def _():
                for half in self.halves(side, hop):
                    self.hop_copy(t, side, hop, half).start()

    def hop_wait_recv(self, t, hop):
        for side in (-1, 1):
            @pl.when(self.has(-side, hop))
            def _():
                for half in self.halves(side, hop):
                    self.hop_copy(t, side, hop, half).wait_recv()

    def hop_wait_send(self, t, hop):
        for side in (-1, 1):
            @pl.when(self.sends(side, hop))
            def _():
                for half in self.halves(side, hop):
                    self.hop_copy(t, side, hop, half).wait_send()

    def weights(self, shift_ref, kernel_ref):
        _, momenta, _, modes = kernel_ref.shape

        def entry(k, carry):
            for q in range(momenta):
                for way in range(2):
                    values = [kernel_ref[way, k, q, m] for m in range(modes)]
                    for distance in range(1, self.span + 1):
                        total = jnp.float32(0.0)
                        for m in range(modes):
                            total = total + jnp.where(shift_ref[m] == distance, values[m], 0.0)
                        self.table[way * self.span + distance - 1, k * momenta + q] = total
            return carry

        lax.fori_loop(0, momenta, entry, 0)

    def mix(self, t):
        cell, chunk = self.steps[t]
        rows = self.field.shape[3]
        tile = 16 if rows % 16 == 0 else 8

        def block(index, carry):
            window = pl.ds(pl.multiple_of(index * tile, tile), tile)
            totals = [[None] * self.momenta for _ in range(2)]
            for offset in range(-self.reach, self.reach + 1):
                for half in range(2):
                    distances = [core - half - 2 * offset for core in range(2)]
                    if all(d == 0 or abs(d) > self.span for d in distances):
                        continue
                    for q in range(self.momenta):
                        value = self.field[t, self.reach + offset, half * self.momenta + q, window]
                        for core, d in enumerate(distances):
                            if d == 0 or abs(d) > self.span:
                                continue
                            row = (0 if d > 0 else self.span) + abs(d) - 1
                            for k in range(self.momenta):
                                term = self.table[row, k * self.momenta + q] * value
                                old = totals[core][k]
                                totals[core][k] = term if old is None else old + term
            for core in range(2):
                for k in range(self.momenta):
                    self.mixed[t, core * self.momenta + k, window] = totals[core][k]
            return carry

        lax.fori_loop(0, rows // tile, block, 0)

    def back_copy(self, t, turn):
        cell, chunk = self.steps[t]
        other = self.partner(turn)
        return pltpu.make_async_remote_copy(
            src_ref=self.mixed.at[t, other],
            dst_ref=self.back.at[cell, self.slot(chunk, self.me)],
            send_sem=self.back_send.at[t, turn],
            recv_sem=self.back_recv.at[t, turn],
            device_id=self.member(other),
            device_id_type=MESH,
        )

    def back_start(self, t):
        for turn in range(1, self.plane):
            self.back_copy(t, turn).start()
        cell, chunk = self.steps[t]
        self.back[cell, self.slot(chunk, self.me)] = self.mixed[t, self.me]

    def store_copy(self, t):
        cell, chunk = self.steps[t]
        rows = self.plane * self.field.shape[3]
        here = pl.ds(chunk * rows, rows)
        return pltpu.make_async_copy(self.back.at[cell, here], self.out.at[here, cell], self.store_sem.at[t])

    def advance(self, s):
        last = len(self.steps)
        if s < last:
            self.plane_wait(s)
            self.hop_start(s, 1)
        for hop in range(2, self.reach + 1):
            t = s - (hop - 1)
            if 0 <= t < last:
                self.hop_wait_recv(t, hop - 1)
                self.hop_start(t, hop)
        t = s - self.reach
        if 0 <= t < last:
            self.hop_wait_recv(t, self.reach)
            self.mix(t)
            self.back_start(t)
        t = s - self.reach - 1
        if 0 <= t < last:
            for turn in range(1, self.plane):
                self.back_copy(t, turn).wait()
            self.store_copy(t).start()

    def finish(self):
        for t in range(len(self.steps)):
            for hop in range(1, self.reach + 1):
                self.hop_wait_send(t, hop)
            self.store_copy(t).wait()


def exchange_scratch(energies, momenta, steps, rows):
    plane, span = 2 * momenta, energies // 2 - 1
    reach = (span + 1) // 2
    dma = pltpu.SemaphoreType.DMA
    return [
        pltpu.VMEM((steps, 2 * reach + 1, plane, rows, LANES), F32),
        pltpu.VMEM((steps, plane, rows, LANES), F32),
        pltpu.SMEM((2 * span, momenta * momenta), F32),
        dma((steps, plane)), dma((steps, plane)),
        dma((steps, 2, reach, 2)), dma((steps, 2, reach, 2)),
        dma((steps, plane)), dma((steps, plane)),
    ]


def chunks_of(cell_rows, plane):
    for chunks in (3, 2, 1):
        if cell_rows % (chunks * plane * 8) == 0:
            return chunks
    raise ValueError("rows")


def split(x):
    high = x.astype(BF16)
    return high, (x - high.astype(F32)).astype(BF16)


def dot(a, b):
    return jnp.dot(a, b, preferred_element_type=F32)


class Point:
    def __init__(self, sizes):
        self.atoms, self.neigh, self.per_atom = sizes
        self.orb = self.atoms * self.per_atom
        self.entries = 2 * self.per_atom * self.per_atom
        self.kinds = 2 * self.per_atom

    def write_left(self, pair, rows, cols, value):
        for ref, part in zip(pair, split(value)):
            ref[rows, cols] = part

    def write_right(self, pair, rows, start, value):
        orb = self.orb
        width = value.shape[1]
        for ref, part in zip(pair, split(value)):
            ref[rows, orb + start:orb + start + width] = part
            cut = max(orb - start, 0)
            if cut < width:
                ref[rows, start + cut - orb:start + width - orb] = -part[:, cut:]

    def product(self, left, right, emit):
        orb = self.orb
        width = 256 if (2 * orb) % 256 == 0 else LANES
        step = 64

        def window(ref, t):
            upper = ref[:, orb + t * width:orb + (t + 1) * width]
            return jnp.concatenate([upper, ref[:, t * width:(t + 1) * width]], axis=0)

        for t in range(2 * orb // width):
            high, low = window(right[0], t), window(right[1], t)
            total = dot(left[0][...], low) + dot(left[1][...], high)
            total = total + dot(left[0][...], high)
            for row in range(0, orb, step):
                emit(slice(row, row + step), t * width, total[row:row + step])

    def index(self, shift_ref):
        place = lax.broadcasted_iota(jnp.int32, (self.neigh, self.atoms), 1) + shift_ref[...]
        return self.per_atom * jnp.where(place >= self.atoms, place - self.atoms, place)

    def prepare_index(self, first, columns_ref, pick_ref):
        group = columns_ref.shape[0]
        each = self.atoms // group
        for g in range(group):
            columns_ref[g, :, 0:each] = first[:, g * each:(g + 1) * each]
        turned = first.T
        wide = jnp.concatenate([turned + j for j in range(self.per_atom)], axis=1)
        used = wide.shape[1]
        for i in range(self.per_atom):
            for start in range(0, used, LANES):
                end = min(start + LANES, used)
                place = pl.ds(i, self.atoms, stride=self.per_atom)
                pick_ref[start // LANES, place, 0:end - start] = wide[:, start:end]

    def turn_pairs(self, pairs_ref, rows_ref, lhs_ref):
        atoms, neigh, per_atom, kinds = self.atoms, self.neigh, self.per_atom, self.kinds
        chunks = neigh * self.entries // LANES
        for cell in range(2):
            for chunk in range(chunks):
                part = pairs_ref[pl.ds(2 * chunk + cell, atoms, stride=2 * chunks), :]
                rows_ref[chunk * LANES:(chunk + 1) * LANES, 0:atoms] = part.T
            for kind in range(kinds):
                parts = [
                    rows_ref[pl.ds(kind * per_atom + j, neigh, stride=self.entries), :] for j in range(per_atom)
                ]
                turned = jnp.concatenate(parts, axis=0)
                for start in range(0, per_atom * neigh, LANES):
                    end = min(start + LANES, per_atom * neigh)
                    place = pl.ds(cell * kinds + kind, atoms, stride=2 * kinds)
                    lhs_ref[start // LANES, place, 0:end - start] = turned[start:end].T[0:atoms]

    def place_pairs(self, columns_ref, lhs_ref, hop_ref, system_ref):
        atoms, neigh, per_atom, orb, kinds = self.atoms, self.neigh, self.per_atom, self.orb, self.kinds
        groups = columns_ref.shape[0]
        each = atoms // groups
        pair = 8 // per_atom
        depth = per_atom * neigh
        lane = lax.broadcasted_iota(jnp.int32, (neigh, LANES), 1)

        def body(g, carry):
            columns = columns_ref[g]
            for u in range(0, each, pair):
                found = []
                for v in range(u, u + pair):
                    column = jnp.broadcast_to(columns[:, v:v + 1], (neigh, LANES))
                    rows = []
                    for j in range(per_atom):
                        tiles = [
                            jnp.where(column == lane + (start - j), 1.0, 0.0).astype(BF16)
                            for start in range(0, orb, LANES)
                        ]
                        rows.append(jnp.concatenate(tiles, axis=1))
                    ones = jnp.concatenate(rows, axis=0)
                    start = pl.multiple_of((g * each + v) * 2 * kinds, 2 * kinds)
                    values = [
                        lhs_ref[begin // LANES, pl.ds(start, 2 * kinds), 0:min(LANES, depth - begin)]
                        for begin in range(0, depth, LANES)
                    ]
                    high, low = split(jnp.concatenate(values, axis=1))
                    both = dot(jnp.concatenate([high, low], axis=0), ones)
                    found.append(both[0:2 * kinds] + both[2 * kinds:])
                here = pl.ds(pl.multiple_of((g * each + u) * per_atom, 8), 8)
                for cell in range(2):
                    for part in range(2):
                        row = cell * kinds + part * per_atom
                        value = jnp.concatenate([f[row:row + per_atom] for f in found], axis=0)
                        system_ref[cell, here, part * orb:(part + 1) * orb] = -(value + hop_ref[0, cell, part, here])
            return carry

        lax.fori_loop(0, groups, body, 0)

    def start_inverse(self, system, level, broadening, left, right, guess):
        orb = self.orb
        step = 32
        row = lax.broadcasted_iota(jnp.int32, (LANES, LANES), 0)
        col = lax.broadcasted_iota(jnp.int32, (LANES, LANES), 1)
        cols = []
        for b in range(orb // LANES):
            here = slice(b * LANES, (b + 1) * LANES)
            there = slice(orb + b * LANES, orb + (b + 1) * LANES)
            real = jnp.sum(jnp.where(row == col, system[here, here] + level[:, here], 0.0), axis=0, keepdims=True)
            imag = jnp.sum(jnp.where(row == col, system[here, there] + broadening, 0.0), axis=0, keepdims=True)
            size = real * real + imag * imag
            cols.append((real / size, -imag / size))
        cr, ci = (jnp.concatenate([c[n] for c in cols], axis=1) for n in range(2))
        for top in range(0, orb, step):
            rows = slice(top, top + step)
            first = top // LANES * LANES
            own = lax.broadcasted_iota(jnp.int32, (step, LANES), 0) + (top - first)
            own = own == lax.broadcasted_iota(jnp.int32, (step, LANES), 1)
            here = slice(first, first + LANES)
            there = slice(orb + first, orb + first + LANES)
            real = jnp.sum(jnp.where(own, system[rows, here] + level[:, here], 0.0), axis=1, keepdims=True)
            imag = jnp.sum(jnp.where(own, system[rows, there] + broadening, 0.0), axis=1, keepdims=True)
            size = real * real + imag * imag
            rr, ri = real / size, -imag / size
            for start in range(0, orb, LANES):
                lanes, after = slice(start, start + LANES), slice(orb + start, orb + start + LANES)
                er, ei = system[rows, lanes], system[rows, after]
                if start == first:
                    er, ei = jnp.where(own, 0.0, er), jnp.where(own, 0.0, ei)
                fr, fi = rr * er - ri * ei, rr * ei + ri * er
                br, bi = cr[:, lanes], ci[:, lanes]
                xr, xi = fi * bi - fr * br, -(fr * bi + fi * br)
                if start == first:
                    xr, xi = xr + jnp.where(own, rr, 0.0), xi + jnp.where(own, ri, 0.0)
                self.write_left(left, rows, lanes, fr)
                self.write_left(left, rows, after, fi)
                self.write_right(right, rows, start, xr)
                self.write_right(right, rows, orb + start, xi)
                guess[rows, lanes] = xr
                guess[rows, after] = xi

    def gather(self, green, pick_ref, taken_ref, rows_ref, store):
        atoms, neigh, per_atom, orb, kinds = self.atoms, self.neigh, self.per_atom, self.orb, self.kinds
        used = per_atom * neigh
        chunks = neigh * self.entries // LANES
        step = 32
        tiles = [(start, min(start + LANES, used)) for start in range(0, used, LANES)]
        for top in range(0, orb, step):
            rows = slice(top, top + step)
            for start, end in tiles:
                pick = pick_ref[start // LANES, rows]
                which, lane = pick // LANES, pick % LANES
                for part in range(2):
                    value = None
                    for source in range(0, orb, LANES):
                        block = green[rows, part * orb + source:part * orb + source + LANES]
                        found = jnp.take_along_axis(block, lane, axis=1)
                        value = found if value is None else jnp.where(which == source // LANES, found, value)
                    taken_ref[part, start // LANES, rows] = value
        extra = jnp.zeros((LANES - atoms, LANES), F32)
        for kind in range(kinds):
            part, i = kind // per_atom, kind % per_atom
            turned = []
            for start, end in tiles:
                block = taken_ref[part, start // LANES, pl.ds(i, atoms, stride=per_atom)]
                turned.append(jnp.concatenate([block, extra], axis=0).T[0:end - start])
            turned = jnp.concatenate(turned, axis=0)
            for j in range(per_atom):
                rows_ref[pl.ds(kind * per_atom + j, neigh, stride=self.entries), :] = turned[j * neigh:(j + 1) * neigh]
        for chunk in range(chunks):
            store(chunk, chunks, rows_ref[chunk * LANES:(chunk + 1) * LANES, :].T[0:atoms])


def point_kernel(
    sizes, dims, shift_ref, kernel_ref, neighbor_ref, onsite_ref, pairs_hbm, hop_hbm, coup_hbm, out_hbm,
    pairs_ref, hop_ref, coup_ref, rows_ref, lhs_ref, columns_ref, pick_ref, taken_ref,
    system, guess, first_green, full,
    lf_h, lf_l, la_h, la_l, lb_h, lb_l, lg_h, lg_l,
    rx_h, rx_l, ry_h, ry_l, rv_h, rv_l, rb_h, rb_l,
    load_sem, store_sem, green, back, *exchange_refs,
):
    field, mixed, table, *sems = exchange_refs
    ex = Exchange(dims, green, back, out_hbm, field, mixed, table, sems, store_sem)
    point = Point(sizes)
    orb = point.orb
    lf, la, lb, lg = (lf_h, lf_l), (la_h, la_l), (lb_h, lb_l), (lg_h, lg_l)
    rx, ry, rv, rb = (rx_h, rx_l), (ry_h, ry_l), (rv_h, rv_l), (rb_h, rb_l)

    loads = [
        pltpu.make_async_copy(src, dst, load_sem.at[n])
        for n, (src, dst) in enumerate(((pairs_hbm, pairs_ref), (hop_hbm, hop_ref), (coup_hbm, coup_ref)))
    ]
    for load in loads:
        load.start()
    ex.announce()
    first = point.index(neighbor_ref)
    point.prepare_index(first, columns_ref, pick_ref)
    ex.weights(shift_ref, kernel_ref)
    ex.blank()
    loads[0].wait()
    point.turn_pairs(pairs_ref, rows_ref, lhs_ref)
    loads[1].wait()
    point.place_pairs(columns_ref, lhs_ref, hop_ref, system)
    loads[2].wait()

    for top in range(0, orb, LANES):
        rows = slice(top, top + LANES)
        for part in range(2):
            value = coup_ref[0, part, rows, :]
            point.write_right(rv, rows, part * orb, value)
            turned = value.T
            if part:
                turned = -turned
            point.write_left(la, slice(0, orb), slice(part * orb + top, part * orb + top + LANES), turned)

    energy_real = 2.0 * (lax.axis_index("energy").astype(F32) + 0.5) / ex.energies

    def finish_inverse(cell, emit):
        level = energy_real - onsite_ref[cell:cell + 1, :]
        point.start_inverse(system.at[cell], level, BROADENING, lf, rx, guess)

        def to_right(rows, start, value):
            point.write_right(ry, rows, start, value)

        point.product(lf, rx, to_right)
        point.product(lf, ry, emit)

    def first_done(rows, start, value):
        cols = slice(start, start + value.shape[1])
        value = guess[rows, cols] + value
        first_green[rows, cols] = value
        point.write_right(rx, rows, start, value)
        point.write_left(lg, rows, cols, value)

    finish_inverse(0, first_done)

    def adjoint_done(rows, start, value):
        point.write_left(lb, rows, slice(start, start + value.shape[1]), value)
        point.write_right(rb, rows, start, value)

    point.product(la, rx, adjoint_done)

    def folded(rows, start, value):
        cols = slice(start, start + value.shape[1])
        system[1, rows, cols] = system[1, rows, cols] - value

    point.product(lb, rv, folded)

    def second_done(rows, start, value):
        cols = slice(start, start + value.shape[1])
        value = guess[rows, cols] + value
        full[rows, cols] = value
        point.write_right(rx, rows, start, value)

    finish_inverse(1, second_done)

    def store_into(cell):
        def store(chunk, chunks, value):
            green[cell, pl.ds(chunk, point.atoms, stride=chunks), :] = value
        return store

    point.gather(full, pick_ref, taken_ref, rows_ref, store_into(1))
    ex.greeted()
    half = ex.chunks
    for t in range(half):
        ex.plane_start(t)

    def to_left(pair):
        def emit(rows, start, value):
            point.write_left(pair, rows, slice(start, start + value.shape[1]), value)
        return emit

    def full_done(rows, start, value):
        cols = slice(start, start + value.shape[1])
        full[rows, cols] = first_green[rows, cols] + value

    done = 0
    for work in (
        lambda: point.product(lg, rv, to_left(lf)),
        lambda: point.product(lf, rx, to_left(lb)),
        lambda: point.product(lb, rb, full_done),
    ):
        work()
        if done < half:
            ex.advance(done)
            done += 1
    point.gather(full, pick_ref, taken_ref, rows_ref, store_into(0))
    for t in range(half, 2 * half):
        ex.plane_start(t)
    for s in range(done, 2 * half + ex.reach + 2):
        ex.advance(s)
    ex.finish()


def points_of(mode_shift, phonon_kernel, neighbor_shift, onsite, pairs, hopping, coupling, energies, momenta):
    neigh, atoms = neighbor_shift.shape
    per_atom = onsite.shape[1] // atoms
    orb = atoms * per_atom
    cell_rows = pairs.shape[0] // 2
    plane = 2 * momenta
    chunks = chunks_of(cell_rows, plane)
    tiles = -(-per_atom * neigh // LANES)
    smem, vmem = pl.BlockSpec(memory_space=pltpu.SMEM), pl.BlockSpec(memory_space=pltpu.VMEM)
    hbm = pl.BlockSpec(memory_space=pl.ANY)
    block = pltpu.VMEM((orb, 2 * orb), F32)
    left = [pltpu.VMEM((orb, 2 * orb), BF16)] * 2
    right = [pltpu.VMEM((orb, 3 * orb), BF16)] * 2
    return pl.pallas_call(
        functools.partial(point_kernel, (atoms, neigh, per_atom), (energies, momenta, chunks)),
        out_shape=jax.ShapeDtypeStruct((cell_rows, 2, LANES), F32),
        in_specs=[smem, smem, vmem, vmem, hbm, hbm, hbm],
        out_specs=hbm,
        scratch_shapes=[
            pltpu.VMEM(pairs.shape, F32),
            pltpu.VMEM(hopping.shape, F32),
            pltpu.VMEM(coupling.shape, F32),
            pltpu.VMEM((cell_rows * LANES // atoms, LANES), F32),
            pltpu.VMEM((tiles, 4 * orb, LANES), F32),
            pltpu.VMEM((atoms // 8, neigh, LANES), jnp.int32),
            pltpu.VMEM((tiles, orb, LANES), jnp.int32),
            pltpu.VMEM((2, tiles, orb, LANES), F32),
            pltpu.VMEM((2, orb, 2 * orb), F32),
        ]
        + [block] * 3
        + left * 4
        + right * 4
        + [pltpu.SemaphoreType.DMA((3,)), pltpu.SemaphoreType.DMA((2 * chunks,))]
        + [pltpu.VMEM((2, cell_rows, LANES), F32)] * 2
        + exchange_scratch(energies, momenta, 2 * chunks, cell_rows // (chunks * plane)),
        compiler_params=pltpu.CompilerParams(
            collective_id=0, has_side_effects=True, vmem_limit_bytes=60 * 1024 * 1024
        ),
        name="point_exchange",
    )(mode_shift, phonon_kernel, neighbor_shift, onsite, pairs, hopping, coupling)


def body(hopping, coupling, onsite, sigma_in, neighbor_shift, mode_shift, phonon_kernel):
    energies = sigma_in.shape[0] * lax.axis_size("energy")
    momenta = sigma_in.shape[1] * lax.axis_size("momentum")
    pair_cols = sigma_in.shape[3]
    pairs = sigma_in.reshape(2, pair_cols // LANES, LANES).transpose(1, 0, 2)
    pairs = pairs.reshape(2 * pair_cols // LANES, LANES)
    mixed = points_of(
        mode_shift, phonon_kernel.transpose(1, 2, 3, 0), neighbor_shift.T, onsite, pairs, hopping, coupling,
        energies, momenta,
    )
    return mixed.transpose(1, 0, 2).reshape(1, 1, 2, pair_cols)


def solution(mesh):
    return jax.shard_map(
        body,
        mesh=mesh,
        in_specs=(
            P("momentum", None, None, None, None),
            P("momentum", None, None, None),
            P(),
            P("energy", "momentum", None, None),
            P(),
            P(),
            P(),
        ),
        out_specs=P("energy", "momentum", None, None),
        check_vma=False,
    )
```

```python
import functools

import jax
import jax.numpy as jnp
from jax import lax
from jax.experimental import pallas as pl
from jax.experimental.pallas import tpu as pltpu
from jax.sharding import PartitionSpec as P

BROADENING = 0.5
LANES = 128
F32 = jnp.float32
BF16 = jnp.bfloat16


MESH = pl.DeviceIdType.MESH


class Exchange:
    def __init__(self, dims, green, back, out, field, mixed, table, sems, store_sem):
        self.energies, self.momenta, self.steps = dims
        self.green, self.back, self.out, self.field = green, back, out, field
        self.mixed, self.table, self.store_sem = mixed, table, store_sem
        self.plane_send, self.plane_recv, self.hop_send, self.hop_recv, self.back_send, self.back_recv = sems
        self.plane = 2 * self.momenta
        self.span = self.energies // 2 - 1
        self.reach = (self.span + 1) // 2
        self.groups = self.energies // 2
        energy, self.k = lax.axis_index("energy"), lax.axis_index("momentum")
        self.group, self.core = energy // 2, energy % 2
        self.me = self.core * self.momenta + self.k
        self.partners = [lax.rem(self.me + turn, self.plane) for turn in range(self.plane)]
        self.members = [self.member(other) for other in self.partners]

    def member(self, index):
        return (2 * self.group + index // self.momenta, index % self.momenta)

    def beside(self, side):
        return (jnp.clip(2 * (self.group + side), 0, self.energies - 2) + self.core, self.k)

    def has(self, side, hops=1):
        other = self.group + side * hops
        return (other >= 0) & (other < self.groups)

    def parts(self, hop):
        near = 2 * hop - 1 <= self.span
        far = 2 * hop <= self.span
        return near, far

    def slot(self, t, owner):
        _, start, rows = self.steps[t]
        return pl.ds(pl.multiple_of(start * self.plane + owner * rows, 8), rows)

    def announce(self):
        barrier = pltpu.get_barrier_semaphore()
        for turn in range(1, self.plane):
            pl.semaphore_signal(barrier, inc=1, device_id=self.members[turn], device_id_type=MESH)
        for side in (-1, 1):
            @pl.when(self.has(side))
            def _():
                pl.semaphore_signal(barrier, inc=1, device_id=self.beside(side), device_id_type=MESH)

    def greeted(self):
        count = self.plane - 1 + self.has(-1).astype(jnp.int32) + self.has(1).astype(jnp.int32)
        pl.semaphore_wait(pltpu.get_barrier_semaphore(), count)

    def blank(self):
        for side in (-1, 1):
            for hop in range(1, self.reach + 1):
                @pl.when(jnp.logical_not(self.has(side, hop)))
                def _():
                    for t in range(len(self.steps)):
                        shape = self.field[t].shape[1:]
                        self.field[t][self.reach + side * hop] = jnp.zeros(shape, F32)

    def plane_copy(self, t, turn):
        cell, _, _ = self.steps[t]
        other = self.partners[turn]
        return pltpu.make_async_remote_copy(
            src_ref=self.green.at[cell, self.slot(t, other)],
            dst_ref=self.field[t].at[self.reach, self.me],
            send_sem=self.plane_send.at[t],
            recv_sem=self.plane_recv.at[t],
            device_id=self.members[turn],
            device_id_type=MESH,
        )

    def plane_start(self, t):
        for turn in range(1, self.plane):
            self.plane_copy(t, turn).start()
        cell, _, _ = self.steps[t]
        self.field[t][self.reach, self.me] = self.green[cell, self.slot(t, self.me)]

    def wait_all(self, t, sems):
        slots = self.mixed[t].at[pl.ds(0, self.plane - 1)]
        pltpu.make_async_copy(slots, slots, sems.at[t]).wait()

    def plane_wait(self, t):
        self.wait_all(t, self.plane_recv)

    def hop_copy(self, t, side, hop, half):
        place = self.reach - side * (hop - 1)
        rows = pl.ds(half * self.momenta, self.momenta)
        index = 0 if side < 0 else 1
        return pltpu.make_async_remote_copy(
            src_ref=self.field[t].at[place, rows],
            dst_ref=self.field[t].at[place - side, rows],
            send_sem=self.hop_send.at[t, index, hop - 1, half],
            recv_sem=self.hop_recv.at[t, index, hop - 1, half],
            device_id=self.beside(side),
            device_id_type=MESH,
        )

    def halves(self, side, hop):
        near, far = self.parts(hop)
        first = 1 if side > 0 else 0
        return [half for half, used in ((first, near), (1 - first, far)) if used]

    def sends(self, side, hop):
        return self.has(side) & self.has(-side, hop - 1)

    def hop_start(self, t, hop):
        for side in (-1, 1):
            @pl.when(self.sends(side, hop))
            def _():
                for half in self.halves(side, hop):
                    self.hop_copy(t, side, hop, half).start()

    def hop_wait_recv(self, t, hop):
        for side in (-1, 1):
            @pl.when(self.has(-side, hop))
            def _():
                for half in self.halves(side, hop):
                    self.hop_copy(t, side, hop, half).wait_recv()

    def hop_wait_send(self, t, hop):
        for side in (-1, 1):
            @pl.when(self.sends(side, hop))
            def _():
                for half in self.halves(side, hop):
                    self.hop_copy(t, side, hop, half).wait_send()

    def weights(self, shift_ref, kernel_ref):
        _, momenta, _, modes = kernel_ref.shape

        def entry(k, carry):
            for q in range(momenta):
                for way in range(2):
                    values = [kernel_ref[way, k, q, m] for m in range(modes)]
                    for distance in range(1, self.span + 1):
                        total = jnp.float32(0.0)
                        for m in range(modes):
                            total = total + jnp.where(shift_ref[m] == distance, values[m], 0.0)
                        self.table[way * self.span + distance - 1, k * momenta + q] = total
            return carry

        lax.fori_loop(0, momenta, entry, 0)

    def mix(self, t):
        cell, _, _ = self.steps[t]
        rows = self.steps[t][2]
        tile = 16 if rows % 16 == 0 else 8

        def block(index, carry):
            window = pl.ds(pl.multiple_of(index * tile, tile), tile)
            totals = [[None] * self.momenta for _ in range(2)]
            for offset in range(-self.reach, self.reach + 1):
                for half in range(2):
                    distances = [core - half - 2 * offset for core in range(2)]
                    if all(d == 0 or abs(d) > self.span for d in distances):
                        continue
                    for q in range(self.momenta):
                        value = self.field[t][self.reach + offset, half * self.momenta + q, window]
                        for core, d in enumerate(distances):
                            if d == 0 or abs(d) > self.span:
                                continue
                            row = (0 if d > 0 else self.span) + abs(d) - 1
                            for k in range(self.momenta):
                                term = self.table[row, k * self.momenta + q] * value
                                old = totals[core][k]
                                totals[core][k] = term if old is None else old + term
            for core in range(2):
                for k in range(self.momenta):
                    self.mixed[t][core * self.momenta + k, window] = totals[core][k]
            return carry

        lax.fori_loop(0, rows // tile, block, 0)

    def back_copy(self, t, turn):
        cell, _, _ = self.steps[t]
        other = self.partners[turn]
        return pltpu.make_async_remote_copy(
            src_ref=self.mixed[t].at[other],
            dst_ref=self.back.at[cell, self.slot(t, self.me)],
            send_sem=self.back_send.at[t],
            recv_sem=self.back_recv.at[t],
            device_id=self.members[turn],
            device_id_type=MESH,
        )

    def back_start(self, t):
        for turn in range(1, self.plane):
            self.back_copy(t, turn).start()
        cell, _, _ = self.steps[t]
        self.back[cell, self.slot(t, self.me)] = self.mixed[t][self.me]

    def store_copy(self, t):
        cell, start, rows = self.steps[t]
        here = pl.ds(start * self.plane, rows * self.plane)
        return pltpu.make_async_copy(self.back.at[cell, here], self.out.at[here, cell], self.store_sem.at[t])

    def valid(self, t):
        return 0 <= t < len(self.steps)

    def share(self, t):
        if self.valid(t):
            self.plane_wait(t)
            self.hop_start(t, 1)

    def forward(self, t, hop):
        if self.valid(t):
            self.hop_wait_recv(t, hop - 1)
            self.hop_start(t, hop)

    def answer(self, t):
        if self.valid(t):
            self.hop_wait_recv(t, self.reach)
            self.mix(t)
            self.back_start(t)

    def keep(self, t):
        if self.valid(t):
            self.wait_all(t, self.back_recv)
            self.store_copy(t).start()

    def advance(self, s):
        for hop in range(2, self.reach + 1):
            self.forward(s - hop + 1, hop)
        self.answer(s - self.reach)
        self.keep(s - self.reach - 1)

    def finish(self):
        for t in range(len(self.steps)):
            for hop in range(1, self.reach + 1):
                self.hop_wait_send(t, hop)
            self.wait_all(t, self.plane_send)
            self.wait_all(t, self.back_send)
            self.store_copy(t).wait()


def exchange_scratch(energies, momenta, steps):
    plane, span = 2 * momenta, energies // 2 - 1
    reach, count = (span + 1) // 2, len(steps)
    dma = pltpu.SemaphoreType.DMA
    return (
        [pltpu.VMEM((2 * reach + 1, plane, rows, LANES), F32) for _, _, rows in steps]
        + [pltpu.VMEM((plane, rows, LANES), F32) for _, _, rows in steps]
        + [
            pltpu.SMEM((2 * span, momenta * momenta), F32),
            dma((count,)), dma((count,)),
            dma((count, 2, reach, 2)), dma((count, 2, reach, 2)),
            dma((count,)), dma((count,)),
        ]
    )


PARTS = (1 / 6, 1 / 2, 1)


def steps_of(cell_rows, plane):
    units = cell_rows // (plane * 8)
    if units * plane * 8 != cell_rows:
        raise ValueError("rows")
    cuts = sorted({0} | {round(units * part) for part in PARTS})
    steps = [(1, 8 * a, 8 * (b - a)) for a, b in zip(cuts, cuts[1:])]
    back = [units - cut for cut in reversed(cuts)]
    return tuple(steps + [(0, 8 * a, 8 * (b - a)) for a, b in zip(back, back[1:])])


def split(x):
    high = x.astype(BF16)
    return high, (x - high.astype(F32)).astype(BF16)


def dot(a, b):
    return jnp.dot(a, b, preferred_element_type=F32)


class Point:
    def __init__(self, sizes):
        self.atoms, self.neigh, self.per_atom = sizes
        self.orb = self.atoms * self.per_atom
        self.entries = 2 * self.per_atom * self.per_atom
        self.kinds = 2 * self.per_atom

    def write_left(self, pair, rows, cols, value):
        for ref, part in zip(pair, split(value)):
            ref[rows, cols] = part

    def write_right(self, pair, rows, start, value):
        orb = self.orb
        width = value.shape[1]
        for ref, part in zip(pair, split(value)):
            ref[rows, orb + start:orb + start + width] = part
            cut = max(orb - start, 0)
            if cut < width:
                ref[rows, start + cut - orb:start + width - orb] = -part[:, cut:]

    def product(self, left, right, emit):
        orb = self.orb
        width = 256 if (2 * orb) % 256 == 0 else LANES
        step = orb // 2

        def window(ref, t):
            upper = ref[:, orb + t * width:orb + (t + 1) * width]
            return jnp.concatenate([upper, ref[:, t * width:(t + 1) * width]], axis=0)

        for t in range(2 * orb // width):
            high, low = window(right[0], t), window(right[1], t)
            for top in range(0, orb, step):
                rows = slice(top, top + step)
                upper, lower = left[0][rows, :], left[1][rows, :]
                total = dot(upper, low) + dot(lower, high)
                emit(rows, t * width, total + dot(upper, high))

    def index(self, shift_ref):
        place = lax.broadcasted_iota(jnp.int32, (self.neigh, self.atoms), 1) + shift_ref[...]
        return self.per_atom * jnp.where(place >= self.atoms, place - self.atoms, place)

    def prepare_index(self, first, columns_ref, pick_ref):
        group = columns_ref.shape[0]
        each = self.atoms // group
        for g in range(group):
            columns_ref[g, :, 0:each] = (first[:, g * each:(g + 1) * each] // self.per_atom).astype(F32)
        turned = first.T
        wide = jnp.concatenate([turned + j for j in range(self.per_atom)], axis=1)
        used = wide.shape[1]
        for i in range(self.per_atom):
            for start in range(0, used, LANES):
                end = min(start + LANES, used)
                place = pl.ds(i, self.atoms, stride=self.per_atom)
                pick_ref[start // LANES, place, 0:end - start] = wide[:, start:end]

    def turn_pairs(self, pairs_ref, rows_ref, lhs_ref):
        atoms, neigh, per_atom, kinds = self.atoms, self.neigh, self.per_atom, self.kinds
        chunks = neigh * self.entries // LANES
        for cell in range(2):
            for chunk in range(chunks):
                part = pairs_ref[pl.ds(2 * chunk + cell, atoms, stride=2 * chunks), :]
                rows_ref[chunk * LANES:(chunk + 1) * LANES, 0:atoms] = part.T
            for kind in range(kinds):
                parts = [
                    rows_ref[pl.ds(kind * per_atom + j, neigh, stride=self.entries), :] for j in range(per_atom)
                ]
                turned = jnp.concatenate(parts, axis=0)
                for start in range(0, per_atom * neigh, LANES):
                    end = min(start + LANES, per_atom * neigh)
                    place = pl.ds(cell * kinds + kind, atoms, stride=2 * kinds)
                    lhs_ref[start // LANES, place, 0:end - start] = turned[start:end].T[0:atoms]

    def place_pairs(self, columns_ref, lhs_ref, hop_ref, system_ref):
        atoms, neigh, per_atom, orb, kinds = self.atoms, self.neigh, self.per_atom, self.orb, self.kinds
        groups = columns_ref.shape[0]
        each = atoms // groups
        pair = 8 // per_atom
        depth = per_atom * neigh
        lane = lax.broadcasted_iota(jnp.int32, (neigh, LANES), 1)
        marks = []
        for j in range(per_atom):
            for start in range(0, orb, LANES):
                mine = (lane - j + per_atom) % per_atom == 0
                mark = jnp.where(mine, (lane - j) // per_atom + start // per_atom, -1)
                marks.append(mark.astype(F32).astype(BF16))
        one, zero = jnp.ones((neigh, LANES), BF16), jnp.zeros((neigh, LANES), BF16)

        def body(g, carry):
            columns = columns_ref[g]
            for u in range(0, each, pair):
                found = []
                for v in range(u, u + pair):
                    column = jnp.broadcast_to(columns[:, v:v + 1], (neigh, LANES)).astype(BF16)
                    rows = []
                    for j in range(per_atom):
                        tiles = [
                            jnp.where(column == marks[j * (orb // LANES) + start // LANES], one, zero)
                            for start in range(0, orb, LANES)
                        ]
                        rows.append(jnp.concatenate(tiles, axis=1))
                    ones = jnp.concatenate(rows, axis=0)
                    start = pl.multiple_of((g * each + v) * 2 * kinds, 2 * kinds)
                    values = [
                        lhs_ref[begin // LANES, pl.ds(start, 2 * kinds), 0:min(LANES, depth - begin)]
                        for begin in range(0, depth, LANES)
                    ]
                    high, low = split(jnp.concatenate(values, axis=1))
                    both = dot(jnp.concatenate([high, low], axis=0), ones)
                    found.append(both[0:2 * kinds] + both[2 * kinds:])
                here = pl.ds(pl.multiple_of((g * each + u) * per_atom, 8), 8)
                for cell in range(2):
                    for part in range(2):
                        row = cell * kinds + part * per_atom
                        value = jnp.concatenate([f[row:row + per_atom] for f in found], axis=0)
                        system_ref[cell, here, part * orb:(part + 1) * orb] = -(value + hop_ref[0, cell, part, here])
            return carry

        lax.fori_loop(0, groups, body, 0, unroll=6)

    def start_inverse(self, system, level, broadening, left, right, guess):
        orb = self.orb
        step = 32
        row = lax.broadcasted_iota(jnp.int32, (LANES, LANES), 0)
        col = lax.broadcasted_iota(jnp.int32, (LANES, LANES), 1)
        cols = []
        for b in range(orb // LANES):
            here = slice(b * LANES, (b + 1) * LANES)
            there = slice(orb + b * LANES, orb + (b + 1) * LANES)
            real = jnp.sum(jnp.where(row == col, system[here, here] + level[:, here], 0.0), axis=0, keepdims=True)
            imag = jnp.sum(jnp.where(row == col, system[here, there] + broadening, 0.0), axis=0, keepdims=True)
            size = real * real + imag * imag
            cols.append((real / size, -imag / size))
        cr, ci = (jnp.concatenate([c[n] for c in cols], axis=1) for n in range(2))
        for top in range(0, orb, step):
            rows = slice(top, top + step)
            first = top // LANES * LANES
            own = lax.broadcasted_iota(jnp.int32, (step, LANES), 0) + (top - first)
            own = own == lax.broadcasted_iota(jnp.int32, (step, LANES), 1)
            here = slice(first, first + LANES)
            there = slice(orb + first, orb + first + LANES)
            real = jnp.sum(jnp.where(own, system[rows, here] + level[:, here], 0.0), axis=1, keepdims=True)
            imag = jnp.sum(jnp.where(own, system[rows, there] + broadening, 0.0), axis=1, keepdims=True)
            size = real * real + imag * imag
            rr, ri = real / size, -imag / size
            for start in range(0, orb, LANES):
                lanes, after = slice(start, start + LANES), slice(orb + start, orb + start + LANES)
                er, ei = system[rows, lanes], system[rows, after]
                if start == first:
                    er, ei = jnp.where(own, 0.0, er), jnp.where(own, 0.0, ei)
                fr, fi = rr * er - ri * ei, rr * ei + ri * er
                br, bi = cr[:, lanes], ci[:, lanes]
                xr, xi = fi * bi - fr * br, -(fr * bi + fi * br)
                if start == first:
                    xr, xi = xr + jnp.where(own, rr, 0.0), xi + jnp.where(own, ri, 0.0)
                self.write_left(left, rows, lanes, fr)
                self.write_left(left, rows, after, fi)
                self.write_right(right, rows, start, xr)
                self.write_right(right, rows, orb + start, xi)
                guess[rows, lanes] = xr
                guess[rows, after] = xi

    def gather(self, green, pick_ref, taken_ref, rows_ref, store):
        atoms, neigh, per_atom, orb, kinds = self.atoms, self.neigh, self.per_atom, self.orb, self.kinds
        used = per_atom * neigh
        chunks = neigh * self.entries // LANES
        step = 32
        tiles = [(start, min(start + LANES, used)) for start in range(0, used, LANES)]
        for top in range(0, orb, step):
            rows = slice(top, top + step)
            for start, end in tiles:
                pick = pick_ref[start // LANES, rows]
                which, lane = pick // LANES, pick % LANES
                for part in range(2):
                    value = None
                    for source in range(0, orb, LANES):
                        block = green[rows, part * orb + source:part * orb + source + LANES]
                        found = jnp.take_along_axis(block, lane, axis=1)
                        value = found if value is None else jnp.where(which == source // LANES, found, value)
                    taken_ref[part, start // LANES, rows] = value
        extra = jnp.zeros((LANES - atoms, LANES), F32)
        for kind in range(kinds):
            part, i = kind // per_atom, kind % per_atom
            turned = []
            for start, end in tiles:
                block = taken_ref[part, start // LANES, pl.ds(i, atoms, stride=per_atom)]
                turned.append(jnp.concatenate([block, extra], axis=0).T[0:end - start])
            turned = jnp.concatenate(turned, axis=0)
            for j in range(per_atom):
                rows_ref[pl.ds(kind * per_atom + j, neigh, stride=self.entries), :] = turned[j * neigh:(j + 1) * neigh]
        for chunk in range(chunks):
            store(chunk, chunks, rows_ref[chunk * LANES:(chunk + 1) * LANES, :].T[0:atoms])


def point_kernel(
    sizes, dims, shift_ref, kernel_ref, neighbor_ref, onsite_ref, pairs_hbm, hop_hbm, coup_hbm, out_hbm,
    pairs_ref, hop_ref, coup_ref, rows_ref, lhs_ref, columns_ref, pick_ref, taken_ref,
    system, guess, first_green, full,
    lf_h, lf_l, la_h, la_l, lb_h, lb_l, lg_h, lg_l,
    rx_h, rx_l, ry_h, ry_l, rv_h, rv_l, rb_h, rb_l,
    load_sem, store_sem, green, back, *exchange_refs,
):
    count = len(dims[2])
    field, mixed = exchange_refs[:count], exchange_refs[count:2 * count]
    table, *sems = exchange_refs[2 * count:]
    ex = Exchange(dims, green, back, out_hbm, field, mixed, table, sems, store_sem)
    point = Point(sizes)
    orb = point.orb
    lf, la, lb, lg = (lf_h, lf_l), (la_h, la_l), (lb_h, lb_l), (lg_h, lg_l)
    rx, ry, rv, rb = (rx_h, rx_l), (ry_h, ry_l), (rv_h, rv_l), (rb_h, rb_l)

    loads = [
        pltpu.make_async_copy(src, dst, load_sem.at[n])
        for n, (src, dst) in enumerate(((pairs_hbm, pairs_ref), (hop_hbm, hop_ref), (coup_hbm, coup_ref)))
    ]
    for load in loads:
        load.start()
    ex.announce()
    first = point.index(neighbor_ref)
    point.prepare_index(first, columns_ref, pick_ref)
    ex.weights(shift_ref, kernel_ref)
    ex.blank()
    loads[0].wait()
    point.turn_pairs(pairs_ref, rows_ref, lhs_ref)
    loads[1].wait()
    point.place_pairs(columns_ref, lhs_ref, hop_ref, system)
    loads[2].wait()

    for top in range(0, orb, LANES):
        rows = slice(top, top + LANES)
        for part in range(2):
            value = coup_ref[0, part, rows, :]
            point.write_right(rv, rows, part * orb, value)
            turned = value.T
            if part:
                turned = -turned
            point.write_left(la, slice(0, orb), slice(part * orb + top, part * orb + top + LANES), turned)

    energy_real = 2.0 * (lax.axis_index("energy").astype(F32) + 0.5) / ex.energies

    def finish_inverse(cell, emit):
        level = energy_real - onsite_ref[cell:cell + 1, :]
        point.start_inverse(system.at[cell], level, BROADENING, lf, rx, guess)

        def to_right(rows, start, value):
            point.write_right(ry, rows, start, value)

        point.product(lf, rx, to_right)
        point.product(lf, ry, emit)

    def first_done(rows, start, value):
        cols = slice(start, start + value.shape[1])
        value = guess[rows, cols] + value
        first_green[rows, cols] = value
        point.write_right(rx, rows, start, value)
        point.write_left(lg, rows, cols, value)

    finish_inverse(0, first_done)

    def adjoint_done(rows, start, value):
        point.write_left(lb, rows, slice(start, start + value.shape[1]), value)
        point.write_right(rb, rows, start, value)

    point.product(la, rx, adjoint_done)

    def folded(rows, start, value):
        cols = slice(start, start + value.shape[1])
        system[1, rows, cols] = system[1, rows, cols] - value

    point.product(lb, rv, folded)

    def second_done(rows, start, value):
        cols = slice(start, start + value.shape[1])
        value = guess[rows, cols] + value
        full[rows, cols] = value
        point.write_right(rx, rows, start, value)

    finish_inverse(1, second_done)

    def store_into(cell):
        def store(chunk, chunks, value):
            green[cell, pl.ds(chunk, point.atoms, stride=chunks), :] = value
        return store

    point.gather(full, pick_ref, taken_ref, rows_ref, store_into(1))
    ex.greeted()
    half = count // 2
    for t in range(half):
        ex.plane_start(t)

    def to_left(pair):
        def emit(rows, start, value):
            point.write_left(pair, rows, slice(start, start + value.shape[1]), value)
        return emit

    def full_done(rows, start, value):
        cols = slice(start, start + value.shape[1])
        full[rows, cols] = first_green[rows, cols] + value

    point.product(lg, rv, to_left(lf))
    ex.share(0)
    point.product(lf, rx, to_left(lb))
    ex.share(1)
    point.product(lb, rb, full_done)
    for t in range(2, half):
        ex.share(t)
    ex.advance(1)
    point.gather(full, pick_ref, taken_ref, rows_ref, store_into(0))
    for t in range(half, count):
        ex.plane_start(t)
    for s in range(2, half):
        ex.advance(s)
    for s in range(half, count + ex.reach + 1):
        ex.share(s)
        ex.advance(s)
    ex.finish()


def points_of(mode_shift, phonon_kernel, neighbor_shift, onsite, pairs, hopping, coupling, energies, momenta):
    neigh, atoms = neighbor_shift.shape
    per_atom = onsite.shape[1] // atoms
    orb = atoms * per_atom
    cell_rows = pairs.shape[0] // 2
    plane = 2 * momenta
    steps = steps_of(cell_rows, plane)
    tiles = -(-per_atom * neigh // LANES)
    smem, vmem = pl.BlockSpec(memory_space=pltpu.SMEM), pl.BlockSpec(memory_space=pltpu.VMEM)
    hbm = pl.BlockSpec(memory_space=pl.ANY)
    block = pltpu.VMEM((orb, 2 * orb), F32)
    left = [pltpu.VMEM((orb, 2 * orb), BF16)] * 2
    right = [pltpu.VMEM((orb, 3 * orb), BF16)] * 2
    return pl.pallas_call(
        functools.partial(point_kernel, (atoms, neigh, per_atom), (energies, momenta, steps)),
        out_shape=jax.ShapeDtypeStruct((cell_rows, 2, LANES), F32),
        in_specs=[smem, smem, vmem, vmem, hbm, hbm, hbm],
        out_specs=hbm,
        scratch_shapes=[
            pltpu.VMEM(pairs.shape, F32),
            pltpu.VMEM(hopping.shape, F32),
            pltpu.VMEM(coupling.shape, F32),
            pltpu.VMEM((cell_rows * LANES // atoms, LANES), F32),
            pltpu.VMEM((tiles, 4 * orb, LANES), F32),
            pltpu.VMEM((atoms // 8, neigh, LANES), F32),
            pltpu.VMEM((tiles, orb, LANES), jnp.int32),
            pltpu.VMEM((2, tiles, orb, LANES), F32),
            pltpu.VMEM((2, orb, 2 * orb), F32),
        ]
        + [block] * 3
        + left * 4
        + right * 4
        + [pltpu.SemaphoreType.DMA((3,)), pltpu.SemaphoreType.DMA((len(steps),))]
        + [pltpu.VMEM((2, cell_rows, LANES), F32)] * 2
        + exchange_scratch(energies, momenta, steps),
        compiler_params=pltpu.CompilerParams(
            collective_id=0, has_side_effects=True, vmem_limit_bytes=60 * 1024 * 1024
        ),
        name="point_exchange",
    )(mode_shift, phonon_kernel, neighbor_shift, onsite, pairs, hopping, coupling)


def body(hopping, coupling, onsite, sigma_in, neighbor_shift, mode_shift, phonon_kernel):
    energies = sigma_in.shape[0] * lax.axis_size("energy")
    momenta = sigma_in.shape[1] * lax.axis_size("momentum")
    pair_cols = sigma_in.shape[3]
    pairs = sigma_in.reshape(2, pair_cols // LANES, LANES).transpose(1, 0, 2)
    pairs = pairs.reshape(2 * pair_cols // LANES, LANES)
    mixed = points_of(
        mode_shift, phonon_kernel.transpose(1, 2, 3, 0), neighbor_shift.T, onsite, pairs, hopping, coupling,
        energies, momenta,
    )
    return mixed.transpose(1, 0, 2).reshape(1, 1, 2, pair_cols)


def solution(mesh):
    return jax.shard_map(
        body,
        mesh=mesh,
        in_specs=(
            P("momentum", None, None, None, None),
            P("momentum", None, None, None),
            P(),
            P("energy", "momentum", None, None),
            P(),
            P(),
            P(),
        ),
        out_specs=P("energy", "momentum", None, None),
        check_vma=False,
    )
```

```python
import functools

import jax
import jax.numpy as jnp
from jax import lax
from jax.experimental import pallas as pl
from jax.experimental.pallas import tpu as pltpu
from jax.sharding import PartitionSpec as P

BROADENING = 0.5
LANES = 128
F32 = jnp.float32
BF16 = jnp.bfloat16


MESH = pl.DeviceIdType.MESH


class Exchange:
    def __init__(self, dims, green, back, out, field, mixed, table, sems, store_sem):
        self.energies, self.momenta, self.steps = dims
        self.green, self.back, self.out, self.field = green, back, out, field
        self.mixed, self.table, self.store_sem = mixed, table, store_sem
        self.plane_send, self.plane_recv, self.hop_send, self.hop_recv, self.back_send, self.back_recv = sems
        self.plane = 2 * self.momenta
        self.span = self.energies // 2 - 1
        self.reach = (self.span + 1) // 2
        self.groups = self.energies // 2
        energy, self.k = lax.axis_index("energy"), lax.axis_index("momentum")
        self.group, self.core = energy // 2, energy % 2
        self.me = self.core * self.momenta + self.k
        self.partners = [lax.rem(self.me + turn, self.plane) for turn in range(self.plane)]
        self.members = [self.member(other) for other in self.partners]

    def member(self, index):
        return (2 * self.group + index // self.momenta, index % self.momenta)

    def beside(self, side):
        return (jnp.clip(2 * (self.group + side), 0, self.energies - 2) + self.core, self.k)

    def has(self, side, hops=1):
        other = self.group + side * hops
        return (other >= 0) & (other < self.groups)

    def parts(self, hop):
        near = 2 * hop - 1 <= self.span
        far = 2 * hop <= self.span
        return near, far

    def slot(self, t, owner):
        _, start, rows = self.steps[t]
        return pl.ds(pl.multiple_of(start * self.plane + owner * rows, 8), rows)

    def announce(self):
        barrier = pltpu.get_barrier_semaphore()
        for turn in range(1, self.plane):
            pl.semaphore_signal(barrier, inc=1, device_id=self.members[turn], device_id_type=MESH)
        for side in (-1, 1):
            @pl.when(self.has(side))
            def _():
                pl.semaphore_signal(barrier, inc=1, device_id=self.beside(side), device_id_type=MESH)

    def greeted(self):
        count = self.plane - 1 + self.has(-1).astype(jnp.int32) + self.has(1).astype(jnp.int32)
        pl.semaphore_wait(pltpu.get_barrier_semaphore(), count)

    def blank(self):
        for side in (-1, 1):
            for hop in range(1, self.reach + 1):
                @pl.when(jnp.logical_not(self.has(side, hop)))
                def _():
                    for t in range(len(self.steps)):
                        shape = self.field[t].shape[1:]
                        self.field[t][self.reach + side * hop] = jnp.zeros(shape, F32)

    def plane_copy(self, t, turn):
        cell, _, _ = self.steps[t]
        other = self.partners[turn]
        return pltpu.make_async_remote_copy(
            src_ref=self.green.at[cell, self.slot(t, other)],
            dst_ref=self.field[t].at[self.reach, self.me],
            send_sem=self.plane_send.at[t],
            recv_sem=self.plane_recv.at[t],
            device_id=self.members[turn],
            device_id_type=MESH,
        )

    def plane_start(self, t):
        for turn in range(1, self.plane):
            self.plane_copy(t, turn).start()
        cell, _, _ = self.steps[t]
        self.field[t][self.reach, self.me] = self.green[cell, self.slot(t, self.me)]

    def wait_all(self, t, sems):
        slots = self.mixed[t].at[pl.ds(0, self.plane - 1)]
        pltpu.make_async_copy(slots, slots, sems.at[t]).wait()

    def plane_wait(self, t):
        self.wait_all(t, self.plane_recv)

    def hop_copy(self, t, side, hop, half):
        place = self.reach - side * (hop - 1)
        rows = pl.ds(half * self.momenta, self.momenta)
        index = 0 if side < 0 else 1
        return pltpu.make_async_remote_copy(
            src_ref=self.field[t].at[place, rows],
            dst_ref=self.field[t].at[place - side, rows],
            send_sem=self.hop_send.at[t, index, hop - 1, half],
            recv_sem=self.hop_recv.at[t, index, hop - 1, half],
            device_id=self.beside(side),
            device_id_type=MESH,
        )

    def halves(self, side, hop):
        near, far = self.parts(hop)
        first = 1 if side > 0 else 0
        return [half for half, used in ((first, near), (1 - first, far)) if used]

    def sends(self, side, hop):
        return self.has(side) & self.has(-side, hop - 1)

    def hop_start(self, t, hop):
        for side in (-1, 1):
            @pl.when(self.sends(side, hop))
            def _():
                for half in self.halves(side, hop):
                    self.hop_copy(t, side, hop, half).start()

    def hop_wait_recv(self, t, hop):
        for side in (-1, 1):
            @pl.when(self.has(-side, hop))
            def _():
                for half in self.halves(side, hop):
                    self.hop_copy(t, side, hop, half).wait_recv()

    def hop_wait_send(self, t, hop):
        for side in (-1, 1):
            @pl.when(self.sends(side, hop))
            def _():
                for half in self.halves(side, hop):
                    self.hop_copy(t, side, hop, half).wait_send()

    def weights(self, shift_ref, kernel_ref):
        _, momenta, _, modes = kernel_ref.shape

        def entry(k, carry):
            for q in range(momenta):
                for way in range(2):
                    values = [kernel_ref[way, k, q, m] for m in range(modes)]
                    for distance in range(1, self.span + 1):
                        total = jnp.float32(0.0)
                        for m in range(modes):
                            total = total + jnp.where(shift_ref[m] == distance, values[m], 0.0)
                        self.table[way * self.span + distance - 1, k * momenta + q] = total
            return carry

        lax.fori_loop(0, momenta, entry, 0)

    def mix(self, t):
        cell, _, _ = self.steps[t]
        rows = self.steps[t][2]
        tile = 16 if rows % 16 == 0 else 8

        def block(index, carry):
            window = pl.ds(pl.multiple_of(index * tile, tile), tile)
            totals = [[None] * self.momenta for _ in range(2)]
            for offset in range(-self.reach, self.reach + 1):
                for half in range(2):
                    distances = [core - half - 2 * offset for core in range(2)]
                    if all(d == 0 or abs(d) > self.span for d in distances):
                        continue
                    for q in range(self.momenta):
                        value = self.field[t][self.reach + offset, half * self.momenta + q, window]
                        for core, d in enumerate(distances):
                            if d == 0 or abs(d) > self.span:
                                continue
                            row = (0 if d > 0 else self.span) + abs(d) - 1
                            for k in range(self.momenta):
                                term = self.table[row, k * self.momenta + q] * value
                                old = totals[core][k]
                                totals[core][k] = term if old is None else old + term
            for core in range(2):
                for k in range(self.momenta):
                    self.mixed[t][core * self.momenta + k, window] = totals[core][k]
            return carry

        lax.fori_loop(0, rows // tile, block, 0)

    def back_copy(self, t, turn):
        cell, _, _ = self.steps[t]
        other = self.partners[turn]
        return pltpu.make_async_remote_copy(
            src_ref=self.mixed[t].at[other],
            dst_ref=self.back.at[cell, self.slot(t, self.me)],
            send_sem=self.back_send.at[t],
            recv_sem=self.back_recv.at[t],
            device_id=self.members[turn],
            device_id_type=MESH,
        )

    def back_start(self, t):
        for turn in range(1, self.plane):
            self.back_copy(t, turn).start()
        cell, _, _ = self.steps[t]
        self.back[cell, self.slot(t, self.me)] = self.mixed[t][self.me]

    def store_copy(self, t):
        cell, start, rows = self.steps[t]
        here = pl.ds(start * self.plane, rows * self.plane)
        return pltpu.make_async_copy(self.back.at[cell, here], self.out.at[here, cell], self.store_sem.at[t])

    def valid(self, t):
        return 0 <= t < len(self.steps)

    def share(self, t):
        if self.valid(t):
            self.plane_wait(t)
            self.hop_start(t, 1)

    def forward(self, t, hop):
        if self.valid(t):
            self.hop_wait_recv(t, hop - 1)
            self.hop_start(t, hop)

    def answer(self, t):
        if self.valid(t):
            self.hop_wait_recv(t, self.reach)
            self.mix(t)
            self.back_start(t)

    def keep(self, t):
        if self.valid(t):
            self.wait_all(t, self.back_recv)
            self.store_copy(t).start()

    def advance(self, s):
        for hop in range(2, self.reach + 1):
            self.forward(s - hop + 1, hop)
        self.answer(s - self.reach)
        self.keep(s - self.reach - 1)

    def finish(self):
        for t in range(len(self.steps)):
            for hop in range(1, self.reach + 1):
                self.hop_wait_send(t, hop)
            self.wait_all(t, self.plane_send)
            self.wait_all(t, self.back_send)
            self.store_copy(t).wait()


def exchange_scratch(energies, momenta, steps):
    plane, span = 2 * momenta, energies // 2 - 1
    reach, count = (span + 1) // 2, len(steps)
    dma = pltpu.SemaphoreType.DMA
    return (
        [pltpu.VMEM((2 * reach + 1, plane, rows, LANES), F32) for _, _, rows in steps]
        + [pltpu.VMEM((plane, rows, LANES), F32) for _, _, rows in steps]
        + [
            pltpu.SMEM((2 * span, momenta * momenta), F32),
            dma((count,)), dma((count,)),
            dma((count, 2, reach, 2)), dma((count, 2, reach, 2)),
            dma((count,)), dma((count,)),
        ]
    )


FIRST = (1 / 3, 1)
LAST = (4 / 9, 7 / 9, 1)


def steps_of(cell_rows, plane):
    units = cell_rows // (plane * 8)
    if units * plane * 8 != cell_rows:
        raise ValueError("rows")
    steps = []
    for cell, parts in ((1, FIRST), (0, LAST)):
        cuts = sorted({0} | {round(units * part) for part in parts})
        steps.extend((cell, 8 * a, 8 * (b - a)) for a, b in zip(cuts, cuts[1:]))
    return tuple(steps)


def split(x):
    high = x.astype(BF16)
    return high, (x - high.astype(F32)).astype(BF16)


def dot(a, b):
    return jnp.dot(a, b, preferred_element_type=F32)


class Point:
    def __init__(self, sizes):
        self.atoms, self.neigh, self.per_atom = sizes
        self.orb = self.atoms * self.per_atom
        self.entries = 2 * self.per_atom * self.per_atom
        self.kinds = 2 * self.per_atom

    def write_left(self, pair, rows, cols, value):
        for ref, part in zip(pair, split(value)):
            ref[rows, cols] = part

    def write_right(self, pair, rows, start, value):
        orb = self.orb
        width = value.shape[1]
        for ref, part in zip(pair, split(value)):
            ref[rows, orb + start:orb + start + width] = part
            cut = max(orb - start, 0)
            if cut < width:
                ref[rows, start + cut - orb:start + width - orb] = -part[:, cut:]

    def product(self, left, right, emit):
        orb = self.orb
        width = 256 if (2 * orb) % 256 == 0 else LANES
        step = orb // 2

        def window(ref, t):
            upper = ref[:, orb + t * width:orb + (t + 1) * width]
            return jnp.concatenate([upper, ref[:, t * width:(t + 1) * width]], axis=0)

        for t in range(2 * orb // width):
            high, low = window(right[0], t), window(right[1], t)
            for top in range(0, orb, step):
                rows = slice(top, top + step)
                upper, lower = left[0][rows, :], left[1][rows, :]
                total = dot(upper, low) + dot(lower, high)
                emit(rows, t * width, total + dot(upper, high))

    def index(self, shift_ref):
        place = lax.broadcasted_iota(jnp.int32, (self.neigh, self.atoms), 1) + shift_ref[...]
        return self.per_atom * jnp.where(place >= self.atoms, place - self.atoms, place)

    def prepare_index(self, first, columns_ref, pick_ref):
        group = columns_ref.shape[0]
        each = self.atoms // group
        for g in range(group):
            columns_ref[g, :, 0:each] = (first[:, g * each:(g + 1) * each] // self.per_atom).astype(F32)
        turned = first.T
        wide = jnp.concatenate([turned + j for j in range(self.per_atom)], axis=1)
        used = wide.shape[1]
        for i in range(self.per_atom):
            for start in range(0, used, LANES):
                end = min(start + LANES, used)
                place = pl.ds(i, self.atoms, stride=self.per_atom)
                pick_ref[start // LANES, place, 0:end - start] = wide[:, start:end]

    def turn_pairs(self, pairs_ref, rows_ref, lhs_ref):
        atoms, neigh, per_atom, kinds = self.atoms, self.neigh, self.per_atom, self.kinds
        chunks = neigh * self.entries // LANES
        for cell in range(2):
            for chunk in range(chunks):
                part = pairs_ref[pl.ds(2 * chunk + cell, atoms, stride=2 * chunks), :]
                rows_ref[chunk * LANES:(chunk + 1) * LANES, 0:atoms] = part.T
            for kind in range(kinds):
                parts = [
                    rows_ref[pl.ds(kind * per_atom + j, neigh, stride=self.entries), :] for j in range(per_atom)
                ]
                turned = jnp.concatenate(parts, axis=0)
                for start in range(0, per_atom * neigh, LANES):
                    end = min(start + LANES, per_atom * neigh)
                    place = pl.ds(cell * kinds + kind, atoms, stride=2 * kinds)
                    lhs_ref[start // LANES, place, 0:end - start] = turned[start:end].T[0:atoms]

    def place_pairs(self, columns_ref, lhs_ref, hop_ref, system_ref):
        atoms, neigh, per_atom, orb, kinds = self.atoms, self.neigh, self.per_atom, self.orb, self.kinds
        groups = columns_ref.shape[0]
        each = atoms // groups
        pair = 8 // per_atom
        depth = per_atom * neigh
        lane = lax.broadcasted_iota(jnp.int32, (neigh, LANES), 1)
        marks = []
        for j in range(per_atom):
            for start in range(0, orb, LANES):
                mine = (lane - j + per_atom) % per_atom == 0
                mark = jnp.where(mine, (lane - j) // per_atom + start // per_atom, -1)
                marks.append(mark.astype(F32).astype(BF16))
        one, zero = jnp.ones((neigh, LANES), BF16), jnp.zeros((neigh, LANES), BF16)

        def body(g, carry):
            columns = columns_ref[g]
            for u in range(0, each, pair):
                found = []
                for v in range(u, u + pair):
                    column = jnp.broadcast_to(columns[:, v:v + 1], (neigh, LANES)).astype(BF16)
                    rows = []
                    for j in range(per_atom):
                        tiles = [
                            jnp.where(column == marks[j * (orb // LANES) + start // LANES], one, zero)
                            for start in range(0, orb, LANES)
                        ]
                        rows.append(jnp.concatenate(tiles, axis=1))
                    ones = jnp.concatenate(rows, axis=0)
                    start = pl.multiple_of((g * each + v) * 2 * kinds, 2 * kinds)
                    values = [
                        lhs_ref[begin // LANES, pl.ds(start, 2 * kinds), 0:min(LANES, depth - begin)]
                        for begin in range(0, depth, LANES)
                    ]
                    high, low = split(jnp.concatenate(values, axis=1))
                    both = dot(jnp.concatenate([high, low], axis=0), ones)
                    found.append(both[0:2 * kinds] + both[2 * kinds:])
                here = pl.ds(pl.multiple_of((g * each + u) * per_atom, 8), 8)
                for cell in range(2):
                    for part in range(2):
                        row = cell * kinds + part * per_atom
                        value = jnp.concatenate([f[row:row + per_atom] for f in found], axis=0)
                        system_ref[cell, here, part * orb:(part + 1) * orb] = -(value + hop_ref[0, cell, part, here])
            return carry

        lax.fori_loop(0, groups, body, 0, unroll=12)

    def start_inverse(self, system, level, broadening, left, right, guess):
        orb = self.orb
        step = 32
        row = lax.broadcasted_iota(jnp.int32, (LANES, LANES), 0)
        col = lax.broadcasted_iota(jnp.int32, (LANES, LANES), 1)
        cols = []
        for b in range(orb // LANES):
            here = slice(b * LANES, (b + 1) * LANES)
            there = slice(orb + b * LANES, orb + (b + 1) * LANES)
            real = jnp.sum(jnp.where(row == col, system[here, here] + level[:, here], 0.0), axis=0, keepdims=True)
            imag = jnp.sum(jnp.where(row == col, system[here, there] + broadening, 0.0), axis=0, keepdims=True)
            size = real * real + imag * imag
            cols.append((real / size, -imag / size))
        cr, ci = (jnp.concatenate([c[n] for c in cols], axis=1) for n in range(2))
        for top in range(0, orb, step):
            rows = slice(top, top + step)
            first = top // LANES * LANES
            own = lax.broadcasted_iota(jnp.int32, (step, LANES), 0) + (top - first)
            own = own == lax.broadcasted_iota(jnp.int32, (step, LANES), 1)
            here = slice(first, first + LANES)
            there = slice(orb + first, orb + first + LANES)
            real = jnp.sum(jnp.where(own, system[rows, here] + level[:, here], 0.0), axis=1, keepdims=True)
            imag = jnp.sum(jnp.where(own, system[rows, there] + broadening, 0.0), axis=1, keepdims=True)
            size = real * real + imag * imag
            rr, ri = real / size, -imag / size
            for start in range(0, orb, LANES):
                lanes, after = slice(start, start + LANES), slice(orb + start, orb + start + LANES)
                er, ei = system[rows, lanes], system[rows, after]
                if start == first:
                    er, ei = jnp.where(own, 0.0, er), jnp.where(own, 0.0, ei)
                fr, fi = rr * er - ri * ei, rr * ei + ri * er
                br, bi = cr[:, lanes], ci[:, lanes]
                xr, xi = fi * bi - fr * br, -(fr * bi + fi * br)
                if start == first:
                    xr, xi = xr + jnp.where(own, rr, 0.0), xi + jnp.where(own, ri, 0.0)
                self.write_left(left, rows, lanes, fr)
                self.write_left(left, rows, after, fi)
                self.write_right(right, rows, start, xr)
                self.write_right(right, rows, orb + start, xi)
                guess[rows, lanes] = xr
                guess[rows, after] = xi

    def gather(self, green, pick_ref, taken_ref, rows_ref, store, begin, finish):
        atoms = finish - begin
        neigh, per_atom, orb, kinds = self.neigh, self.per_atom, self.orb, self.kinds
        used = per_atom * neigh
        chunks = neigh * self.entries // LANES
        step = 32
        tiles = [(start, min(start + LANES, used)) for start in range(0, used, LANES)]
        for top in range(per_atom * begin, per_atom * finish, step):
            rows = slice(top, top + step)
            for start, end in tiles:
                pick = pick_ref[start // LANES, rows]
                which, lane = pick // LANES, pick % LANES
                for part in range(2):
                    value = None
                    for source in range(0, orb, LANES):
                        block = green[rows, part * orb + source:part * orb + source + LANES]
                        found = jnp.take_along_axis(block, lane, axis=1)
                        value = found if value is None else jnp.where(which == source // LANES, found, value)
                    taken_ref[part, start // LANES, rows] = value
        for kind in range(kinds):
            part, i = kind // per_atom, kind % per_atom
            turned = []
            for start, end in tiles:
                place = pl.ds(per_atom * begin + i, atoms, stride=per_atom)
                turned.append(taken_ref[part, start // LANES, place].T[0:end - start])
            turned = jnp.concatenate(turned, axis=0)
            for j in range(per_atom):
                place = pl.ds(kind * per_atom + j, neigh, stride=self.entries)
                rows_ref[place, 0:atoms] = turned[j * neigh:(j + 1) * neigh]
        for chunk in range(chunks):
            store(begin, chunk, chunks, rows_ref[chunk * LANES:(chunk + 1) * LANES, 0:atoms].T)


def point_kernel(
    sizes, dims, shift_ref, kernel_ref, neighbor_ref, onsite_ref, pairs_hbm, hop_hbm, coup_hbm, out_hbm,
    pairs_ref, hop_ref, coup_ref, rows_ref, lhs_ref, columns_ref, pick_ref, taken_ref,
    system, guess, first_green, full,
    lf_h, lf_l, la_h, la_l, lb_h, lb_l, lg_h, lg_l,
    rx_h, rx_l, ry_h, ry_l, rv_h, rv_l, rb_h, rb_l,
    load_sem, store_sem, green, back, *exchange_refs,
):
    count = len(dims[2])
    field, mixed = exchange_refs[:count], exchange_refs[count:2 * count]
    table, *sems = exchange_refs[2 * count:]
    ex = Exchange(dims, green, back, out_hbm, field, mixed, table, sems, store_sem)
    point = Point(sizes)
    orb = point.orb
    lf, la, lb, lg = (lf_h, lf_l), (la_h, la_l), (lb_h, lb_l), (lg_h, lg_l)
    rx, ry, rv, rb = (rx_h, rx_l), (ry_h, ry_l), (rv_h, rv_l), (rb_h, rb_l)

    loads = [
        pltpu.make_async_copy(src, dst, load_sem.at[n])
        for n, (src, dst) in enumerate(((pairs_hbm, pairs_ref), (hop_hbm, hop_ref), (coup_hbm, coup_ref)))
    ]
    for load in loads:
        load.start()
    ex.announce()
    first = point.index(neighbor_ref)
    point.prepare_index(first, columns_ref, pick_ref)
    ex.weights(shift_ref, kernel_ref)
    ex.blank()
    loads[0].wait()
    point.turn_pairs(pairs_ref, rows_ref, lhs_ref)
    loads[1].wait()
    point.place_pairs(columns_ref, lhs_ref, hop_ref, system)
    loads[2].wait()

    for top in range(0, orb, LANES):
        rows = slice(top, top + LANES)
        for part in range(2):
            value = coup_ref[0, part, rows, :]
            point.write_right(rv, rows, part * orb, value)
            turned = value.T
            if part:
                turned = -turned
            point.write_left(la, slice(0, orb), slice(part * orb + top, part * orb + top + LANES), turned)

    energy_real = 2.0 * (lax.axis_index("energy").astype(F32) + 0.5) / ex.energies

    def finish_inverse(cell, emit):
        level = energy_real - onsite_ref[cell:cell + 1, :]
        point.start_inverse(system.at[cell], level, BROADENING, lf, rx, guess)

        def to_right(rows, start, value):
            point.write_right(ry, rows, start, value)

        point.product(lf, rx, to_right)
        point.product(lf, ry, emit)

    def first_done(rows, start, value):
        cols = slice(start, start + value.shape[1])
        value = guess[rows, cols] + value
        first_green[rows, cols] = value
        point.write_right(rx, rows, start, value)

    finish_inverse(0, first_done)

    def adjoint_done(rows, start, value):
        point.write_left(lb, rows, slice(start, start + value.shape[1]), value)

    point.product(la, rx, adjoint_done)

    def folded(rows, start, value):
        cols = slice(start, start + value.shape[1])
        system[1, rows, cols] = system[1, rows, cols] - value

    point.product(lb, rv, folded)

    def second_done(rows, start, value):
        cols = slice(start, start + value.shape[1])
        value = guess[rows, cols] + value
        full[rows, cols] = value

    finish_inverse(1, second_done)

    def store_into(cell):
        def store(begin, chunk, chunks, value):
            green[cell, pl.ds(begin * chunks + chunk, value.shape[0], stride=chunks), :] = value
        return store

    half = sum(cell for cell, _, _ in ex.steps)
    per_step = ex.plane * point.atoms
    early = -(-ex.steps[0][2] * per_step // (8 * green.shape[1])) * 8
    if early >= point.atoms:
        early = point.atoms
    point.gather(full, pick_ref, taken_ref, rows_ref, store_into(1), 0, early)
    ex.greeted()
    ex.plane_start(0)
    if early < point.atoms:
        point.gather(full, pick_ref, taken_ref, rows_ref, store_into(1), early, point.atoms)
    for t in range(1, half):
        ex.plane_start(t)

    for top in range(0, orb, LANES):
        rows = slice(top, top + LANES)
        for start in range(0, 2 * orb, LANES):
            cols = slice(start, start + LANES)
            point.write_left(lg, rows, cols, first_green[rows, cols])
            point.write_right(rx, rows, start, full[rows, cols])
        for dst, src in zip(rb, lb):
            dst[rows, orb:] = src[rows, :]
            dst[rows, 0:orb] = -src[rows, orb:]

    def to_left(pair):
        def emit(rows, start, value):
            point.write_left(pair, rows, slice(start, start + value.shape[1]), value)
        return emit

    def full_done(rows, start, value):
        cols = slice(start, start + value.shape[1])
        full[rows, cols] = first_green[rows, cols] + value

    point.product(lg, rv, to_left(lf))
    ex.share(0)
    point.product(lf, rx, to_left(lb))
    ex.share(1)
    point.product(lb, rb, full_done)
    for t in range(2, half):
        ex.share(t)
    ex.advance(1)
    point.gather(full, pick_ref, taken_ref, rows_ref, store_into(0), 0, point.atoms)
    for t in range(half, count):
        ex.plane_start(t)
    for s in range(2, half):
        ex.advance(s)
    for s in range(half, count + ex.reach + 1):
        ex.share(s)
        ex.advance(s)
    ex.finish()


def points_of(mode_shift, phonon_kernel, neighbor_shift, onsite, pairs, hopping, coupling, energies, momenta):
    neigh, atoms = neighbor_shift.shape
    per_atom = onsite.shape[1] // atoms
    orb = atoms * per_atom
    cell_rows = pairs.shape[0] // 2
    plane = 2 * momenta
    steps = steps_of(cell_rows, plane)
    tiles = -(-per_atom * neigh // LANES)
    smem, vmem = pl.BlockSpec(memory_space=pltpu.SMEM), pl.BlockSpec(memory_space=pltpu.VMEM)
    hbm = pl.BlockSpec(memory_space=pl.ANY)
    block = pltpu.VMEM((orb, 2 * orb), F32)
    left = [pltpu.VMEM((orb, 2 * orb), BF16)] * 2
    right = [pltpu.VMEM((orb, 3 * orb), BF16)] * 2
    return pl.pallas_call(
        functools.partial(point_kernel, (atoms, neigh, per_atom), (energies, momenta, steps)),
        out_shape=jax.ShapeDtypeStruct((cell_rows, 2, LANES), F32),
        in_specs=[smem, smem, vmem, vmem, hbm, hbm, hbm],
        out_specs=hbm,
        scratch_shapes=[
            pltpu.VMEM(pairs.shape, F32),
            pltpu.VMEM(hopping.shape, F32),
            pltpu.VMEM(coupling.shape, F32),
            pltpu.VMEM((cell_rows * LANES // atoms, LANES), F32),
            pltpu.VMEM((tiles, 4 * orb, LANES), F32),
            pltpu.VMEM((atoms // 8, neigh, LANES), F32),
            pltpu.VMEM((tiles, orb, LANES), jnp.int32),
            pltpu.VMEM((2, tiles, orb, LANES), F32),
            pltpu.VMEM((2, orb, 2 * orb), F32),
        ]
        + [block] * 3
        + left * 4
        + right * 4
        + [pltpu.SemaphoreType.DMA((3,)), pltpu.SemaphoreType.DMA((len(steps),))]
        + [pltpu.VMEM((2, cell_rows, LANES), F32)] * 2
        + exchange_scratch(energies, momenta, steps),
        compiler_params=pltpu.CompilerParams(
            collective_id=0, has_side_effects=True, vmem_limit_bytes=60 * 1024 * 1024
        ),
        name="point_exchange",
    )(mode_shift, phonon_kernel, neighbor_shift, onsite, pairs, hopping, coupling)


def body(hopping, coupling, onsite, sigma_in, neighbor_shift, mode_shift, phonon_kernel):
    energies = sigma_in.shape[0] * lax.axis_size("energy")
    momenta = sigma_in.shape[1] * lax.axis_size("momentum")
    pair_cols = sigma_in.shape[3]
    pairs = sigma_in.reshape(2, pair_cols // LANES, LANES).transpose(1, 0, 2)
    pairs = pairs.reshape(2 * pair_cols // LANES, LANES)
    mixed = points_of(
        mode_shift, phonon_kernel.transpose(1, 2, 3, 0), neighbor_shift.T, onsite, pairs, hopping, coupling,
        energies, momenta,
    )
    return mixed.transpose(1, 0, 2).reshape(1, 1, 2, pair_cols)


def solution(mesh):
    return jax.shard_map(
        body,
        mesh=mesh,
        in_specs=(
            P("momentum", None, None, None, None),
            P("momentum", None, None, None),
            P(),
            P("energy", "momentum", None, None),
            P(),
            P(),
            P(),
        ),
        out_specs=P("energy", "momentum", None, None),
        check_vma=False,
    )
```
